256 devices in a mesh: dp: 8 (over x, y_hi), ctx: 32 (over y_lo, z, core).
Axes of the slice: x: 4, y: 4 (y_hi: 2, y_lo: 2; y = y_hi * 2 + y_lo), z: 8, core: 2. Of those that a mesh axis runs over, the one named last changes fastest.
Arguments:
- projections: bfloat16 [3072, 65536], P(None, ('dp', 'ctx')), may hold values from -6 to 6
- short_filter: bfloat16 [7, 3072], replicated, may hold values from -2 to 2
- long_filter: bfloat16 [256, 65536], P(('dp', 'ctx')), may hold values from -6 to 6
- out_grad: bfloat16 [1024, 65536], P(None, ('dp', 'ctx')), may hold values from -3 to 3
Outputs:
- mixed: bfloat16 [1024, 65536], P(None, ('dp', 'ctx'))
- proj_grad: bfloat16 [3072, 65536], P(None, ('dp', 'ctx'))
- filter_grad: float32 [256, 65536], P(('dp', 'ctx'))
The draws below stay inside these ranges and needn't reach their ends.
All inputs are finite; a program needn't handle non-finite values.
Results may differ from the reference program's by a relative error of at most 0.01.
Values may be sent and summed in bfloat16 or wider, within the bound.
A program may use at most 64 MiB of HBM per device.

```python
import math
import jax
import jax.numpy as jnp
from jax import lax

CH = 1024
CPG = 4
TAPS = 7
SEQ = 65536
GROUPS = 256


def steps_of(rng, extent, cuts, low, largest):
    gain = 1.0
    for position, parts in cuts:
        draws = jax.random.uniform(jax.random.fold_in(jax.random.fold_in(rng, 6), position), (parts,), jnp.float32, low / len(cuts), largest / len(cuts))
        gain = gain * jnp.repeat(jnp.exp(draws), extent[position] // parts).reshape((-1,) + (1,) * (len(extent) - 1 - position))
    return gain


def normal_values(stream_key, extent, spread, bound, shards=(), kind=jnp.bfloat16):
    level = steps_of(stream_key, extent, shards, -0.22, 0.18) if shards else 1.0
    array = jax.random.normal(stream_key, extent, jnp.float32) * spread * level
    return jnp.minimum(jnp.maximum(array, -bound), bound).astype(kind)


def setup_inputs(seed: int = 0) -> dict:
    keys = jax.random.split(jax.random.key(seed), 5)
    projections = normal_values(keys[0], (3 * CH, SEQ), 1.0, 6.0, ((1, 256),))
    short_filter = normal_values(keys[1], (TAPS, 3 * CH), TAPS ** -0.5, 2.0)
    long_filter = normal_values(keys[2], (GROUPS, SEQ), 1.0, 6.0, ((0, 256),))
    out_grad = normal_values(keys[3], (CH, SEQ), 0.5, 3.0, ((1, 256),))
    return {"projections": projections, "short_filter": short_filter, "long_filter": long_filter, "out_grad": out_grad}


def contract(form, first, second):
    return jnp.einsum(form, first.astype(jnp.float32), second.astype(jnp.float32), precision=lax.Precision.HIGHEST)


def rounded(values):
    return lax.optimization_barrier(values.astype(jnp.bfloat16)).astype(jnp.float32)


def dft_table(count_out, count_in, period):
    left_index = jnp.arange(count_out, dtype=jnp.int32)[:, None]
    right_index = jnp.arange(count_in, dtype=jnp.int32)[None, :]
    angle = ((left_index * right_index) % period).astype(jnp.float32) * (2.0 * math.pi / period)
    return jnp.cos(angle), jnp.sin(angle)


def make_tables():
    padded_len = 2 * SEQ
    inner_len = max(divisor for divisor in range(1, SEQ + 1) if SEQ % divisor == 0 and divisor * divisor <= padded_len)
    outer_len = padded_len // inner_len
    cos_outer, sin_outer = dft_table(outer_len, outer_len // 2, outer_len)
    cos_inner, sin_inner = dft_table(inner_len, inner_len, inner_len)
    return ((rounded(cos_outer), rounded(sin_outer)), dft_table(outer_len, inner_len, padded_len), (rounded(cos_inner), rounded(sin_inner)), padded_len)


def forward_dft(signal, tables):
    (cos_outer, sin_outer), (cos_twist, sin_twist), (cos_inner, sin_inner), padded_len = tables
    count = signal.shape[0]
    folded = signal.astype(jnp.float32).reshape(count, cos_outer.shape[1], cos_inner.shape[0])
    first_re = contract("db,rba->rda", cos_outer, folded)
    first_im = -contract("db,rba->rda", sin_outer, folded)
    twist_re = rounded(first_re * cos_twist + first_im * sin_twist)
    twist_im = rounded(first_im * cos_twist - first_re * sin_twist)
    spec_re = contract("rda,ae->rde", twist_re, cos_inner) + contract("rda,ae->rde", twist_im, sin_inner)
    spec_im = contract("rda,ae->rde", twist_im, cos_inner) - contract("rda,ae->rde", twist_re, sin_inner)
    return spec_re, spec_im


def inverse_dft(spec_re, spec_im, tables):
    (cos_outer, sin_outer), (cos_twist, sin_twist), (cos_inner, sin_inner), padded_len = tables
    count = spec_re.shape[0]
    back_re = contract("rde,ea->rda", spec_re, cos_inner) - contract("rde,ea->rda", spec_im, sin_inner)
    back_im = contract("rde,ea->rda", spec_im, cos_inner) + contract("rde,ea->rda", spec_re, sin_inner)
    turn_re = rounded(back_re * cos_twist - back_im * sin_twist)
    turn_im = rounded(back_im * cos_twist + back_re * sin_twist)
    signal = contract("db,rda->rba", cos_outer, turn_re) - contract("db,rda->rba", sin_outer, turn_im)
    return signal.reshape(count, -1) / padded_len


def reference(projections, short_filter, long_filter, out_grad):
    scale = SEQ ** -0.5
    tables = make_tables()
    weights = short_filter.astype(jnp.float32)
    source = projections.astype(jnp.float32)
    total = jnp.zeros((3 * CH, SEQ), jnp.float32)
    for lag in range(TAPS):
        total = total + weights[lag][:, None] * jnp.pad(source, ((0, 0), (lag, 0)))[:, :SEQ]
    features = total.astype(jnp.bfloat16)
    query = features[:CH].astype(jnp.float32)
    key_part = features[CH:2 * CH].astype(jnp.float32)
    value_part = features[2 * CH:].astype(jnp.float32)
    product = (key_part * value_part).astype(jnp.bfloat16)
    cot = out_grad.astype(jnp.float32)
    conv_grad = (cot * query).astype(jnp.bfloat16)

    block_groups = math.gcd(GROUPS, 16)
    block_count = GROUPS // block_groups
    block_chan = block_groups * CPG

    def per_block(triple):
        prod_block, grad_block, filt_block = triple
        filt_re, filt_im = forward_dft(filt_block, tables)
        filt_re = filt_re[:, None]
        filt_im = filt_im[:, None]
        prod_re, prod_im = forward_dft(prod_block, tables)
        grad_re, grad_im = forward_dft(grad_block, tables)
        shape = (block_groups, CPG) + prod_re.shape[1:]
        prod_re = prod_re.reshape(shape)
        prod_im = prod_im.reshape(shape)
        grad_re = grad_re.reshape(shape)
        grad_im = grad_im.reshape(shape)
        flat = (-1,) + prod_re.shape[2:]
        conv_re = rounded((filt_re * prod_re - filt_im * prod_im) * scale).reshape(flat)
        conv_im = rounded((filt_re * prod_im + filt_im * prod_re) * scale).reshape(flat)
        conv = inverse_dft(conv_re, conv_im, tables).astype(jnp.bfloat16)
        back_re = rounded((filt_re * grad_re + filt_im * grad_im) * scale).reshape(flat)
        back_im = rounded((filt_re * grad_im - filt_im * grad_re) * scale).reshape(flat)
        back = inverse_dft(back_re, back_im, tables).astype(jnp.bfloat16)
        cross_re = rounded(jnp.sum(prod_re * grad_re + prod_im * grad_im, axis=1))
        cross_im = rounded(jnp.sum(prod_re * grad_im - prod_im * grad_re, axis=1))
        filter_part = inverse_dft(cross_re, cross_im, tables) * scale
        return conv, back, filter_part

    conv_b, back_b, filter_b = lax.map(per_block, (product.reshape(block_count, block_chan, SEQ), conv_grad.reshape(block_count, block_chan, SEQ), long_filter.reshape(block_count, block_groups, SEQ)))
    conv = conv_b.reshape(CH, SEQ).astype(jnp.float32)
    back = back_b.reshape(CH, SEQ).astype(jnp.float32)
    filter_grad = filter_b.reshape(GROUPS, SEQ)
    mixed = (query * conv).astype(jnp.bfloat16)
    query_grad = (cot * conv).astype(jnp.bfloat16)
    key_grad = (back * value_part).astype(jnp.bfloat16)
    value_grad = (back * key_part).astype(jnp.bfloat16)
    feat_grad = jnp.concatenate([query_grad, key_grad, value_grad], axis=0).astype(jnp.float32)
    gathered = jnp.zeros((3 * CH, SEQ), jnp.float32)
    for lag in range(TAPS):
        gathered = gathered + weights[lag][:, None] * jnp.pad(feat_grad, ((0, 0), (0, lag)))[:, lag:]
    return mixed, gathered.astype(jnp.bfloat16), filter_grad
```

```python
import math

import jax
import jax.numpy as jnp
from jax import lax
from jax.experimental import pallas as pl
from jax.experimental.pallas import tpu as pltpu
from jax.sharding import PartitionSpec as P

CPG = 4
TAPS = 7
LANES = 32


def place(index):
    return (index // LANES, index % LANES)


def signal(sem, index):
    pl.semaphore_signal(sem, inc=1, device_id=place(index), device_id_type=pl.DeviceIdType.MESH)


def enter(rounds):
    me = lax.axis_index("dp") * LANES + lax.axis_index("ctx")
    high, low = me // 16, me % 16
    gate = pltpu.get_barrier_semaphore()
    for step in range(1, 16):
        signal(gate, high * 16 + (low + step) % 16)
    for step in range(1, 16):
        signal(gate, ((high + step) % 16) * 16 + low)
    pl.semaphore_wait(gate, 30)
    for step in range(1, 16):
        signal(rounds.at[0], high * 16 + (low + step) % 16)
    pl.semaphore_wait(rounds.at[0], 15)
    for step in range(1, 16):
        signal(rounds.at[1], ((high + step) % 16) * 16 + low)
    pl.semaphore_wait(rounds.at[1], 15)


def remote(source, target, sems, index):
    return pltpu.make_async_remote_copy(source, target, sems.at[0], sems.at[1], device_id=place(index), device_id_type=pl.DeviceIdType.MESH)


def exchange_kernel(out_ref, in_ref, mid, rounds, swap, own, wide):
    me = lax.axis_index("dp") * LANES + lax.axis_index("ctx")
    chip, core = me // 2, me % 2
    enter(rounds)
    swapped = remote(out_ref.at[:, 1 - core], mid.at[:, core], swap, chip * 2 + 1 - core)
    swapped.start()
    kept = pltpu.make_async_copy(out_ref.at[:, core], mid.at[:, core], own.at[0])
    kept.start()
    kept.wait()
    swapped.wait()

    def send(step, carry):
        other = (chip + step) % 128
        remote(mid.at[other], in_ref.at[chip], wide, other * 2 + core).start()
        return carry

    lax.fori_loop(1, 128, send, 0)
    stay = pltpu.make_async_copy(mid.at[chip], in_ref.at[chip], own.at[1])
    stay.start()
    stay.wait()
    arrived = remote(mid.at[pl.ds(0, 127)], in_ref.at[pl.ds(0, 127)], wide, ((chip + 1) % 128) * 2 + core)
    arrived.wait_send()
    arrived.wait_recv()


def exchange(blocks):
    shape = (128, 2) + blocks.shape[1:]
    moved = pl.pallas_call(
        exchange_kernel,
        out_shape=jax.ShapeDtypeStruct(shape, blocks.dtype),
        in_specs=[pl.BlockSpec(memory_space=pltpu.VMEM)],
        out_specs=pl.BlockSpec(memory_space=pltpu.VMEM),
        scratch_shapes=[
            pltpu.VMEM(shape, blocks.dtype),
            pltpu.SemaphoreType.REGULAR((2,)),
            pltpu.SemaphoreType.DMA((2,)),
            pltpu.SemaphoreType.DMA((2,)),
            pltpu.SemaphoreType.DMA((2,)),
        ],
        compiler_params=pltpu.CompilerParams(collective_id=0, has_side_effects=True, vmem_limit_bytes=32 << 20),
    )(blocks.reshape(shape))
    return moved.reshape(blocks.shape)


def shifted(value, axis, steps):
    count = lax.axis_size(axis)
    first, last = (max(0, -steps), min(count, count - steps))
    return lax.ppermute(value, axis, [(source, source + steps) for source in range(first, last)])


def contract(form, first, second):
    return jnp.einsum(form, first, second, preferred_element_type=jnp.float32)


def dft_table(count_out, count_in, period):
    left_index = jnp.arange(count_out, dtype=jnp.int32)[:, None]
    right_index = jnp.arange(count_in, dtype=jnp.int32)[None, :]
    angle = (left_index * right_index % period).astype(jnp.float32) * (2.0 * math.pi / period)
    return (jnp.cos(angle), jnp.sin(angle))


def make_tables(seq_len):
    padded_len = 2 * seq_len
    inner_len = max(
        (
            divisor
            for divisor in range(1, seq_len + 1)
            if seq_len % divisor == 0 and divisor * divisor <= padded_len
        )
    )
    outer_len = padded_len // inner_len
    cos_outer, sin_outer = dft_table(outer_len, outer_len // 2, outer_len)
    cos_inner, sin_inner = dft_table(inner_len, inner_len, inner_len)
    return (
        (cos_outer.astype(jnp.bfloat16), sin_outer.astype(jnp.bfloat16)),
        dft_table(outer_len, inner_len, padded_len),
        (cos_inner.astype(jnp.bfloat16), sin_inner.astype(jnp.bfloat16)),
        padded_len,
    )


def forward_dft(signal, tables):
    (cos_outer, sin_outer), (cos_twist, sin_twist), (cos_inner, sin_inner), padded_len = tables
    count = signal.shape[0]
    folded = signal.reshape(count, cos_outer.shape[1], cos_inner.shape[0])
    first_re = contract("db,rba->rda", cos_outer, folded)
    first_im = -contract("db,rba->rda", sin_outer, folded)
    twist_re = (first_re * cos_twist + first_im * sin_twist).astype(jnp.bfloat16)
    twist_im = (first_im * cos_twist - first_re * sin_twist).astype(jnp.bfloat16)
    spec_re = contract("rda,ae->rde", twist_re, cos_inner) + contract(
        "rda,ae->rde", twist_im, sin_inner
    )
    spec_im = contract("rda,ae->rde", twist_im, cos_inner) - contract(
        "rda,ae->rde", twist_re, sin_inner
    )
    return (spec_re, spec_im)


def inverse_dft(spec_re, spec_im, tables):
    (cos_outer, sin_outer), (cos_twist, sin_twist), (cos_inner, sin_inner), padded_len = tables
    count = spec_re.shape[0]
    back_re = contract("rde,ea->rda", spec_re, cos_inner) - contract(
        "rde,ea->rda", spec_im, sin_inner
    )
    back_im = contract("rde,ea->rda", spec_im, cos_inner) + contract(
        "rde,ea->rda", spec_re, sin_inner
    )
    turn_re = (back_re * cos_twist - back_im * sin_twist).astype(jnp.bfloat16)
    turn_im = (back_im * cos_twist + back_re * sin_twist).astype(jnp.bfloat16)
    signal = contract("db,rda->rba", cos_outer, turn_re) - contract(
        "db,rda->rba", sin_outer, turn_im
    )
    return signal.reshape(count, -1) / padded_len


def shards(projections, short_filter, long_filter, out_grad):
    width = out_grad.shape[0]
    local_len = out_grad.shape[1]
    lanes_dp = lax.axis_size("dp")
    lanes_ctx = lax.axis_size("ctx")
    seq_len = local_len * lanes_dp * lanes_ctx
    groups = width // CPG
    local_groups = long_filter.shape[0]
    tables = make_tables(seq_len)
    weights = short_filter.astype(jnp.float32)
    rim_len = TAPS - 1
    earlier = shifted(projections[:, local_len - rim_len :], ("dp", "ctx"), 1)
    extended = jnp.concatenate([earlier, projections], axis=1).astype(jnp.float32)
    total = jnp.zeros(projections.shape, jnp.float32)
    for lag in range(TAPS):
        total = (
            total + weights[lag][:, None] * extended[:, rim_len - lag : rim_len - lag + local_len]
        )
    features = total.astype(jnp.bfloat16)
    query = features[:width].astype(jnp.float32)
    key_part = features[width : 2 * width].astype(jnp.float32)
    value_part = features[2 * width :].astype(jnp.float32)
    product = (key_part * value_part).astype(jnp.bfloat16)
    cotangent = out_grad.astype(jnp.float32)
    conv_grad = (cotangent * query).astype(jnp.bfloat16)
    scale = seq_len ** (-0.5)
    filt_re, filt_im = forward_dft(long_filter, tables)
    filt_re = filt_re[:, None]
    filt_im = filt_im[:, None]

    def spectra(whole):
        spec_re, spec_im = forward_dft(whole.reshape(-1, seq_len), tables)
        shape = (local_groups, CPG) + spec_re.shape[1:]
        return (spec_re.reshape(shape), spec_im.reshape(shape))

    def inverse_block(spec_re, spec_im):
        flat_shape = (-1,) + spec_re.shape[2:]
        signal = inverse_dft(spec_re.reshape(flat_shape), spec_im.reshape(flat_shape), tables)
        return signal.reshape(local_groups, CPG, seq_len).astype(jnp.bfloat16)

    both = jnp.concatenate([product.reshape(groups, CPG, local_len), conv_grad.reshape(groups, CPG, local_len)], axis=1)
    both = exchange(both).transpose(1, 0, 2)
    prod_re, prod_im = spectra(both[:CPG])
    conv_re = ((filt_re * prod_re - filt_im * prod_im) * scale).astype(jnp.bfloat16)
    conv_im = ((filt_re * prod_im + filt_im * prod_re) * scale).astype(jnp.bfloat16)
    conv_chan = inverse_block(conv_re, conv_im)
    grad_re, grad_im = spectra(both[CPG:])
    back_re = ((filt_re * grad_re + filt_im * grad_im) * scale).astype(jnp.bfloat16)
    back_im = ((filt_re * grad_im - filt_im * grad_re) * scale).astype(jnp.bfloat16)
    back_chan = inverse_block(back_re, back_im)
    back_both = jnp.concatenate([conv_chan.reshape(CPG, -1, local_len), back_chan.reshape(CPG, -1, local_len)], axis=0)
    back_both = exchange(back_both.transpose(1, 0, 2))
    conv_tok = back_both[:, :CPG]
    back_tok = back_both[:, CPG:]
    cross_re = jnp.sum(prod_re * grad_re + prod_im * grad_im, axis=1).astype(jnp.bfloat16)
    cross_im = jnp.sum(prod_re * grad_im - prod_im * grad_re, axis=1).astype(jnp.bfloat16)
    filter_grad = inverse_dft(cross_re, cross_im, tables) * scale
    conv = conv_tok.reshape(width, local_len).astype(jnp.float32)
    back = back_tok.reshape(width, local_len).astype(jnp.float32)
    mixed = (query * conv).astype(jnp.bfloat16)
    query_grad = (cotangent * conv).astype(jnp.bfloat16)
    key_grad = (back * value_part).astype(jnp.bfloat16)
    value_grad = (back * key_part).astype(jnp.bfloat16)
    feat_grad = jnp.concatenate([query_grad, key_grad, value_grad], axis=0)
    later = shifted(feat_grad[:, :rim_len], ("dp", "ctx"), -1)
    extended_grad = jnp.concatenate([feat_grad, later], axis=1).astype(jnp.float32)
    gathered = jnp.zeros(projections.shape, jnp.float32)
    for lag in range(TAPS):
        gathered = gathered + weights[lag][:, None] * extended_grad[:, lag : lag + local_len]
    proj_grad = gathered.astype(jnp.bfloat16)
    return (mixed, proj_grad, filter_grad)


def solution(mesh):
    placed = (P(None, ("dp", "ctx")), P(), P(("dp", "ctx"), None), P(None, ("dp", "ctx")))
    return jax.shard_map(
        shards,
        mesh=mesh,
        in_specs=placed,
        out_specs=(P(None, ("dp", "ctx")), P(None, ("dp", "ctx")), P(("dp", "ctx"), None)),
        check_vma=False,
    )
```

```python
import functools
import math

import jax
import jax.numpy as jnp
import numpy as np
from jax import lax
from jax.experimental import pallas as pl
from jax.experimental.pallas import tpu as pltpu
from jax.sharding import PartitionSpec as P

CPG = 4
TAPS = 7
LANES = 32
CH = 1024
SEQ = 65536
PAD = 2 * SEQ
A = 256
B = 512
HALF = 256
ROWS = 272
CHIPS = 128
DEVICES = 256
SCALE = SEQ ** -0.5
BLOCK = 512
NT = (((1,), (1,)), ((), ()))
TN = (((0,), (0,)), ((), ()))
F32 = jnp.float32
BF16 = jnp.bfloat16


def make_tables():
    order = np.concatenate([np.arange(0, HALF, 2), np.arange(1, HALF, 2)])
    d = np.arange(HALF)[:, None]
    outer = 2 * np.pi * ((d * order[None, :]) % B) / B
    cos_outer, sin_outer = np.cos(outer), np.sin(outer)
    sign = 1.0 - 2.0 * (order % 2)
    spread = np.zeros((2 * HALF + 16, HALF))
    spread[:HALF] = cos_outer
    spread[HALF : 2 * HALF] = -sin_outer
    spread[2 * HALF] = sign
    gather = np.zeros((HALF, 2 * HALF))
    gather[:, :HALF] = 2 * cos_outer.T
    gather[:, 0] = 1.0
    gather[:, HALF:] = -2 * sin_outer.T
    gather[:, HALF] = sign
    e = np.arange(A)
    inner = 2 * np.pi * ((e[:, None] * e[None, :]) % A) / A
    cos_inner, sin_inner = np.cos(inner), np.sin(inner)
    mix = np.block([[cos_inner, -sin_inner], [sin_inner, cos_inner]])
    twist = 2 * np.pi * (np.arange(ROWS)[:, None] * e[None, :]) / PAD
    return (
        jnp.asarray(spread.astype(np.float32), BF16),
        jnp.asarray(gather.astype(np.float32), BF16),
        jnp.asarray(mix.astype(np.float32), BF16),
        jnp.asarray(np.cos(twist).astype(np.float32)),
        jnp.asarray(np.sin(twist).astype(np.float32)),
    )


def place(index):
    return (index // LANES, index % LANES)


def signal(sem, index):
    pl.semaphore_signal(sem, inc=1, device_id=place(index), device_id_type=pl.DeviceIdType.MESH)


def remote(source, target, sems, index):
    return pltpu.make_async_remote_copy(
        source, target, sems.at[0], sems.at[1], device_id=place(index), device_id_type=pl.DeviceIdType.MESH
    )


def dot(first, second):
    return jnp.dot(first, second, preferred_element_type=F32)


def one_hot(shape, offset, limit):
    row = lax.broadcasted_iota(jnp.int32, shape, 0)
    lane = lax.broadcasted_iota(jnp.int32, shape, 1)
    return ((lane == row + offset) & (row < limit)).astype(F32).astype(BF16)


def mixer_kernel(
    proj, taps, filt, grad, spread, gather, mix, cos_twist, sin_twist,
    mixed, pgrad, fgrad,
    weights, shift, feat, prod, cotp, recv_p, recv_g, fold, signals, swap_out, swap_in, kept, ready_c, ready_b, tok_c, tok_b,
    fspec, kspec, cross, bins, rows, mixback, dfeat, edge_out, edge_in, edge_q,
    rounds, sem_edge, sem_edge_q, sem_edge_kv, sem_p, sem_g, sem_c, sem_b, swap_p, swap_g, swap_c, swap_b, own,
):
    me = lax.axis_index("dp") * LANES + lax.axis_index("ctx")
    chip, core = me // 2, me % 2
    high, low = me // 16, me % 16
    twin = chip * 2 + 1 - core
    after, before = (me + 1) % DEVICES, (me + DEVICES - 1) % DEVICES
    mine = pl.ds(pl.multiple_of(core * CHIPS, CHIPS), CHIPS)
    theirs = pl.ds(pl.multiple_of((1 - core) * CHIPS, CHIPS), CHIPS)

    gate = pltpu.get_barrier_semaphore()
    for step in range(1, 16):
        signal(gate, high * 16 + (low + step) % 16)
    for step in range(1, 16):
        signal(gate, ((high + step) % 16) * 16 + low)
    signal(gate, after)
    signal(gate, before)

    last = one_hot((16, A), A - TAPS + 1, TAPS - 1)
    first = one_hot((16, A), 0, TAPS - 1)
    for block in range(0, 3 * CH, BLOCK):
        edge_out[0, :, block : block + BLOCK] = lax.dot_general(
            last, proj[block : block + BLOCK, :], NT, preferred_element_type=F32
        ).astype(BF16)
    for block in range(0, 3 * CH, 128):
        weights[block : block + 128, :] = jnp.transpose(taps[:, block : block + 128])
    row = lax.broadcasted_iota(jnp.int32, (A, 128), 0)
    lane = lax.broadcasted_iota(jnp.int32, (A, 128), 1)
    for lag in range(1, TAPS):
        span = slice((lag - 1) * 128, lag * 128)
        shift[0, :, span] = (row == lane + 128 - lag).astype(F32).astype(BF16)
        shift[1, :, span] = (row == lane + lag).astype(F32).astype(BF16)
    mixback[:A, :A] = mix[:A, :A]
    mixback[A:, A:] = mix[A:, A:]
    mixback[:A, A:] = mix[A:, :A]
    mixback[A:, :A] = mix[:A, A:]

    def forward(signal_rows):
        raw = dot(spread[...], signal_rows)
        re, im, odd = raw[:HALF], raw[HALF : 2 * HALF], raw[2 * HALF :]
        ct, st = cos_twist[:HALF, :], sin_twist[:HALF, :]
        bins[:HALF, :A] = (re * ct + im * st).astype(BF16)
        bins[:HALF, A:] = (im * ct - re * st).astype(BF16)
        bins[HALF:, :A] = (odd * cos_twist[HALF:, :]).astype(BF16)
        bins[HALF:, A:] = (-odd * sin_twist[HALF:, :]).astype(BF16)
        return dot(bins[...], mix[...])

    def inverse(re, im):
        bins[:, :A] = re.astype(BF16)
        bins[:, A:] = im.astype(BF16)
        back = dot(bins[...], mixback[...])
        re, im = back[:, :A], back[:, A:]
        ct, st = cos_twist[...], sin_twist[...]
        turn_re = re * ct - im * st
        turn_im = im[:HALF] * ct[:HALF] + re[:HALF] * st[:HALF]
        top = lax.broadcasted_iota(jnp.int32, (16, A), 0) == 0
        rows[:HALF, :] = turn_re[:HALF].astype(BF16)
        rows[HALF:, :] = turn_im.astype(BF16)
        rows[HALF : HALF + 16, :] = jnp.where(top, turn_re[HALF:], turn_im[:16]).astype(BF16)
        return dot(gather[...], rows[...]) * (1.0 / PAD)

    pl.semaphore_wait(gate, 32)
    edge = remote(edge_out.at[0], edge_in.at[0], sem_edge, after)
    edge.start()
    for step in range(1, 16):
        signal(rounds.at[0], high * 16 + (low + step) % 16)

    for half in range(2):
        lanes = slice(half * 128, half * 128 + 128)
        fold[half, :HALF, :] = filt[:, lanes].astype(F32)
        for parity in range(2):
            rows[parity * CHIPS : (parity + 1) * CHIPS, lanes] = fold[
                half, pl.ds(parity, CHIPS, stride=2), :
            ].astype(BF16)
    fspec[...] = forward(rows[:HALF, :])

    pl.semaphore_wait(rounds.at[0], 15)
    for step in range(1, 16):
        signal(rounds.at[1], ((high + step) % 16) * 16 + low)

    edge.wait()
    ahead = one_hot((16, 128), 128 - TAPS + 1, TAPS - 1)
    behind = one_hot((16, 128), 0, TAPS - 1)

    def filtered(start):
        span = pl.ds(pl.multiple_of(start, BLOCK), BLOCK)
        prior = lax.dot_general(edge_in[0, :, span], ahead, TN, preferred_element_type=F32).astype(BF16)
        prior = jnp.where(me > 0, prior, jnp.zeros_like(prior))
        block = proj[span, :]
        scale = weights[span, :]
        halves = []
        for half, window in ((0, jnp.concatenate([prior, block[:, :128]], axis=1)), (1, block)):
            moved = dot(window, shift[0])
            total = scale[:, 0:1] * block[:, half * 128 : half * 128 + 128].astype(F32)
            for lag in range(1, TAPS):
                total = total + scale[:, lag : lag + 1] * moved[:, (lag - 1) * 128 : lag * 128]
            total = total.astype(BF16)
            feat[span, half * 128 : half * 128 + 128] = total
            halves.append(total.astype(F32))
        return halves

    def make_product(step, carry):
        keys = filtered(CH + step * BLOCK)
        values = filtered(2 * CH + step * BLOCK)
        for half in range(2):
            both = (keys[half] * values[half]).reshape(BLOCK // 8, 8, 128)
            prod[pl.ds(step * (BLOCK // 8), BLOCK // 8), :, half * 128 : half * 128 + 128] = both.astype(BF16)
        return carry

    def make_cotangent(step, carry):
        queries = filtered(step * BLOCK)
        span = pl.ds(pl.multiple_of(step * BLOCK, BLOCK), BLOCK)
        for half in range(2):
            lanes = slice(half * 128, half * 128 + 128)
            both = (queries[half] * grad[span, lanes].astype(F32)).reshape(BLOCK // 8, 8, 128)
            cotp[pl.ds(step * (BLOCK // 8), BLOCK // 8), :, lanes] = both.astype(BF16)
        return carry

    def send_all(source, target, sems, slot):
        def send(step, carry):
            other = (chip + step) % CHIPS
            remote(source.at[other], target.at[chip], sems, other * 2 + core).start()
            return carry

        lax.fori_loop(1, CHIPS, send, 0)
        keep = pltpu.make_async_copy(source.at[chip], target.at[chip], own.at[slot])
        keep.start()
        return keep

    def settle(source, target, sems, keep):
        keep.wait()
        others = pl.ds(0, CHIPS - 1)
        whole = remote(source.at[others], target.at[others], sems, ((chip + 1) % CHIPS) * 2 + core)
        whole.wait_send()
        whole.wait_recv()

    lax.fori_loop(0, CH // BLOCK, make_product, 0)
    pl.semaphore_wait(rounds.at[1], 15)
    keep_p = send_all(prod, recv_p, sem_p, 0)
    lax.fori_loop(0, CH // BLOCK, make_cotangent, 0)
    keep_g = send_all(cotp, recv_g, sem_g, 1)

    def unfold(received, stream, swap):
        for half in range(2):
            lanes = slice(half * 128, half * 128 + 128)
            fold[half] = received[:, :, lanes].astype(F32).reshape(CHIPS * 8, 128)
            for channel in range(CPG):
                low_set = fold[half, pl.ds(channel, CHIPS, stride=8), :]
                high_set = fold[half, pl.ds(CPG + channel, CHIPS, stride=8), :]
                signals[stream * CPG + channel, mine, lanes] = jnp.where(core == 0, low_set, high_set).astype(BF16)
                swap_out[stream, channel, :, lanes] = jnp.where(core == 0, high_set, low_set).astype(BF16)
        moved = remote(
            swap_out.at[stream], signals.at[pl.ds(stream * CPG, CPG), mine, :], swap, twin
        )
        moved.start()
        moved.wait()

    def refold(stream, ready, swap):
        moved = remote(swap_out.at[2 + stream], swap_in.at[stream], swap, twin)
        moved.start()
        moved.wait()
        for half in range(2):
            lanes = slice(half * 128, half * 128 + 128)
            for channel in range(CPG):
                here = kept[stream, channel, :, lanes].astype(F32)
                there = swap_in[stream, channel, :, lanes].astype(F32)
                fold[half, pl.ds(channel, CHIPS, stride=8), :] = jnp.where(core == 0, here, there)
                fold[half, pl.ds(CPG + channel, CHIPS, stride=8), :] = jnp.where(core == 0, there, here)
            ready[:, :, lanes] = fold[half].reshape(CHIPS, 8, 128).astype(BF16)

    def put_away(result, stream, channel):
        even, odd = result[:CHIPS], result[CHIPS:]
        kept[stream, channel] = jnp.where(core == 0, even, odd).astype(BF16)
        swap_out[2 + stream, channel] = jnp.where(core == 0, odd, even).astype(BF16)

    settle(prod, recv_p, sem_p, keep_p)
    unfold(recv_p, 0, swap_p)

    def convolve(channel, carry):
        spec = forward(signals[channel])
        kspec[channel] = spec
        re, im = spec[:, :A], spec[:, A:]
        f_re, f_im = fspec[:, :A], fspec[:, A:]
        put_away(inverse((f_re * re - f_im * im) * SCALE, (f_re * im + f_im * re) * SCALE), 0, channel)
        return carry

    lax.fori_loop(0, CPG, convolve, 0)
    refold(0, ready_c, swap_c)
    keep_c = send_all(ready_c, tok_c, sem_c, 2)

    settle(cotp, recv_g, sem_g, keep_g)
    unfold(recv_g, 1, swap_g)
    cross[...] = jnp.zeros_like(cross)

    def correlate(channel, carry):
        spec = forward(signals[CPG + channel])
        re, im = spec[:, :A], spec[:, A:]
        k_re, k_im = kspec[channel, :, :A], kspec[channel, :, A:]
        cross[:, :A] = cross[:, :A] + (k_re * re + k_im * im)
        cross[:, A:] = cross[:, A:] + (k_re * im - k_im * re)
        f_re, f_im = fspec[:, :A], fspec[:, A:]
        put_away(inverse((f_re * re + f_im * im) * SCALE, (f_re * im - f_im * re) * SCALE), 1, channel)
        return carry

    lax.fori_loop(0, CPG, correlate, 0)
    refold(1, ready_b, swap_b)
    keep_b = send_all(ready_b, tok_b, sem_b, 3)

    result = inverse(cross[:, :A], cross[:, A:]) * SCALE
    for parity in range(2):
        for half in range(2):
            fold[half, pl.ds(parity, CHIPS, stride=2), :] = result[
                parity * CHIPS : (parity + 1) * CHIPS, half * 128 : half * 128 + 128
            ]
    for half in range(2):
        fgrad[:, half * 128 : half * 128 + 128] = fold[half, :HALF, :]

    settle(ready_c, tok_c, sem_c, keep_c)

    def use_conv(step, carry):
        span = pl.ds(pl.multiple_of(step * BLOCK, BLOCK), BLOCK)
        conv = tok_c[pl.ds(step * (BLOCK // 8), BLOCK // 8)].astype(F32).reshape(BLOCK, A)
        mixed[span, :] = (feat[span, :].astype(F32) * conv).astype(BF16)
        back = (grad[span, :].astype(F32) * conv).astype(BF16)
        dfeat[span, :] = back
        edge_q[0, :, span] = lax.dot_general(first, back, NT, preferred_element_type=F32).astype(BF16)
        return carry

    lax.fori_loop(0, CH // BLOCK, use_conv, 0)
    edge_back = remote(edge_q.at[0], edge_q.at[1], sem_edge_q, before)
    edge_back.start()
    edge_back.wait()

    def gathered(start, halo):
        span = pl.ds(pl.multiple_of(start, BLOCK), BLOCK)
        later = lax.dot_general(halo, behind, TN, preferred_element_type=F32).astype(BF16)
        later = jnp.where(me < DEVICES - 1, later, jnp.zeros_like(later))
        block = dfeat[span, :]
        scale = weights[span, :]
        for half, window in ((0, block), (1, jnp.concatenate([block[:, 128:], later], axis=1))):
            lanes = slice(half * 128, half * 128 + 128)
            moved = dot(window, shift[1])
            total = scale[:, 0:1] * block[:, lanes].astype(F32)
            for lag in range(1, TAPS):
                total = total + scale[:, lag : lag + 1] * moved[:, (lag - 1) * 128 : lag * 128]
            pgrad[span, lanes] = total.astype(BF16)

    def finish_query(step, carry):
        gathered(step * BLOCK, edge_q[1, :, pl.ds(pl.multiple_of(step * BLOCK, BLOCK), BLOCK)])
        return carry

    lax.fori_loop(0, CH // BLOCK, finish_query, 0)
    settle(ready_b, tok_b, sem_b, keep_b)

    def use_back(step, carry):
        back = tok_b[pl.ds(step * (BLOCK // 8), BLOCK // 8)].astype(F32).reshape(BLOCK, A)
        for part, other in ((1, 2), (2, 1)):
            source = pl.ds(pl.multiple_of(other * CH + step * BLOCK, BLOCK), BLOCK)
            target = pl.ds(pl.multiple_of(part * CH + step * BLOCK, BLOCK), BLOCK)
            result = (feat[source, :].astype(F32) * back).astype(BF16)
            dfeat[target, :] = result
            edge_out[1, :, target] = lax.dot_general(first, result, NT, preferred_element_type=F32).astype(BF16)
        return carry

    lax.fori_loop(0, CH // BLOCK, use_back, 0)
    tail = pl.ds(CH, 2 * CH)
    edge_last = remote(edge_out.at[1, :, tail], edge_in.at[1, :, tail], sem_edge_kv, before)
    edge_last.start()
    edge_last.wait()

    def finish_rest(step, carry):
        gathered(CH + step * BLOCK, edge_in[1, :, pl.ds(pl.multiple_of(CH + step * BLOCK, BLOCK), BLOCK)])
        return carry

    lax.fori_loop(0, 2 * CH // BLOCK, finish_rest, 0)


def shards(projections, short_filter, long_filter, out_grad):
    taps = jnp.pad(short_filter.astype(F32), ((0, 8 - TAPS), (0, 0)))
    vmem = pl.BlockSpec(memory_space=pltpu.VMEM)
    tokens = pltpu.VMEM((CHIPS, 8, A), BF16)
    pair = pltpu.SemaphoreType.DMA((2,))
    mixed, proj_grad, filter_grad = pl.pallas_call(
        mixer_kernel,
        out_shape=(
            jax.ShapeDtypeStruct((CH, A), BF16),
            jax.ShapeDtypeStruct((3 * CH, A), BF16),
            jax.ShapeDtypeStruct((HALF, A), F32),
        ),
        in_specs=[vmem] * 9,
        out_specs=(vmem, vmem, vmem),
        scratch_shapes=[
            pltpu.VMEM((3 * CH, 8), F32),
            pltpu.VMEM((2, A, 128 * (TAPS - 1)), BF16),
            pltpu.VMEM((3 * CH, A), BF16),
            tokens, tokens, tokens, tokens,
            pltpu.VMEM((2, CHIPS * 8, 128), F32),
            pltpu.VMEM((2 * CPG, HALF, A), BF16),
            pltpu.VMEM((4, CPG, CHIPS, A), BF16),
            pltpu.VMEM((2, CPG, CHIPS, A), BF16),
            pltpu.VMEM((2, CPG, CHIPS, A), BF16),
            tokens, tokens, tokens, tokens,
            pltpu.VMEM((ROWS, 2 * A), F32),
            pltpu.VMEM((CPG, ROWS, 2 * A), F32),
            pltpu.VMEM((ROWS, 2 * A), F32),
            pltpu.VMEM((ROWS, 2 * A), BF16),
            pltpu.VMEM((2 * HALF, A), BF16),
            pltpu.VMEM((2 * A, 2 * A), BF16),
            pltpu.VMEM((3 * CH, A), BF16),
            pltpu.VMEM((2, 16, 3 * CH), BF16),
            pltpu.VMEM((2, 16, 3 * CH), BF16),
            pltpu.VMEM((2, 16, CH), BF16),
            pltpu.SemaphoreType.REGULAR((2,)),
            pair, pair, pair, pair, pair, pair, pair, pair, pair, pair, pair,
            pltpu.SemaphoreType.DMA((4,)),
        ],
        compiler_params=pltpu.CompilerParams(collective_id=0, has_side_effects=True, vmem_limit_bytes=60 << 20),
        name="mixer",
    )(projections, taps, long_filter.reshape(HALF, A), out_grad, *make_tables())
    return (mixed, proj_grad, filter_grad.reshape(1, SEQ))


def solution(mesh):
    placed = (P(None, ("dp", "ctx")), P(), P(("dp", "ctx"), None), P(None, ("dp", "ctx")))
    return jax.shard_map(
        shards,
        mesh=mesh,
        in_specs=placed,
        out_specs=(P(None, ("dp", "ctx")), P(None, ("dp", "ctx")), P(("dp", "ctx"), None)),
        check_vma=False,
    )
```

```python
import functools
import math

import jax
import jax.numpy as jnp
import numpy as np
from jax import lax
from jax.experimental import pallas as pl
from jax.experimental.pallas import tpu as pltpu
from jax.sharding import PartitionSpec as P

CPG = 4
TAPS = 7
LANES = 32
CH = 1024
SEQ = 65536
PAD = 2 * SEQ
A = 256
B = 512
HALF = 256
ROWS = 272
CHIPS = 128
DEVICES = 256
SCALE = SEQ ** -0.5
BLOCK = 512
SIDE = 64
NT = (((1,), (1,)), ((), ()))
TN = (((0,), (0,)), ((), ()))
F32 = jnp.float32
BF16 = jnp.bfloat16


def make_tables():
    order = np.concatenate([np.arange(0, HALF, 2), np.arange(1, HALF, 2)])
    d = np.arange(HALF)[:, None]
    outer = 2 * np.pi * ((d * order[None, :]) % B) / B
    cos_outer, sin_outer = np.cos(outer), np.sin(outer)
    sign = 1.0 - 2.0 * (order % 2)
    spread = np.zeros((2 * HALF + 16, HALF))
    spread[:HALF] = cos_outer
    spread[HALF : 2 * HALF] = -sin_outer
    spread[2 * HALF] = sign
    gather = np.zeros((HALF, 2 * HALF))
    gather[:, :HALF] = 2 * cos_outer.T
    gather[:, 0] = 1.0
    gather[:, HALF:] = -2 * sin_outer.T
    gather[:, HALF] = sign
    e = np.arange(A)
    inner = 2 * np.pi * ((e[:, None] * e[None, :]) % A) / A
    cos_inner, sin_inner = np.cos(inner), np.sin(inner)
    mix = np.block([[cos_inner, -sin_inner], [sin_inner, cos_inner]])
    twist = 2 * np.pi * (np.arange(ROWS)[:, None] * e[None, :]) / PAD
    return (
        jnp.asarray(spread.astype(np.float32), BF16),
        jnp.asarray(gather.astype(np.float32), BF16),
        jnp.asarray(mix.astype(np.float32), BF16),
        jnp.asarray(np.cos(twist).astype(np.float32)),
        jnp.asarray(np.sin(twist).astype(np.float32)),
    )


def place(index):
    return (index // LANES, index % LANES)


def signal(sem, index):
    pl.semaphore_signal(sem, inc=1, device_id=place(index), device_id_type=pl.DeviceIdType.MESH)


def remote(source, target, sems, index):
    return pltpu.make_async_remote_copy(
        source, target, sems.at[0], sems.at[1], device_id=place(index), device_id_type=pl.DeviceIdType.MESH
    )


def dot(first, second):
    return jnp.dot(first, second, preferred_element_type=F32)


def one_hot(shape, offset, limit):
    row = lax.broadcasted_iota(jnp.int32, shape, 0)
    lane = lax.broadcasted_iota(jnp.int32, shape, 1)
    return ((lane == row + offset) & (row < limit)).astype(F32).astype(BF16)


def mixer_kernel(
    proj_hbm, taps_hbm, filt_hbm, grad_hbm, spread_hbm, gather_hbm, mix_hbm, cos_hbm, sin_hbm,
    mixed, pgrad, fgrad,
    proj, taps, filt, grad, spread, gather, mix, cos_twist, sin_twist, padded,
    weights, shift, feat, prod, cotp, recv_p, recv_g, fold, signals, swap_out, swap_in, kept, ready_c, ready_b, tok_c, tok_b,
    fspec, kspec, cross, bins, rows, mixback, dfeat, edge_out, edge_in, edge_q,
    rounds, loads, sem_edge, sem_edge_q, sem_edge_own, sem_edge_rest, sem_first, sem_p, sem_g, sem_c, sem_b,
    swap_p, swap_g, swap_c, swap_b, own,
):
    me = lax.axis_index("dp") * LANES + lax.axis_index("ctx")
    chip, core = me // 2, me % 2
    high, low = me // 16, me % 16
    side, within = chip // SIDE, chip % SIDE
    twin = chip * 2 + 1 - core
    after, before = (me + 1) % DEVICES, (me + DEVICES - 1) % DEVICES
    mine = pl.ds(pl.multiple_of(core * CHIPS, CHIPS), CHIPS)

    def channels(part, turn):
        return pl.multiple_of(part * CH + (side * (1 - turn) + (1 - side) * turn) * BLOCK, BLOCK)

    def load(source, target, slot):
        copy = pltpu.make_async_copy(source, target, loads.at[slot])
        copy.start()
        return copy

    taps_load = load(taps_hbm, taps, 0)
    parts = {}
    for slot, (part, turn) in enumerate(((1, 0), (2, 0), (1, 1), (2, 1), (0, 0), (0, 1))):
        span = pl.ds(channels(part, turn), BLOCK)
        parts[part, turn] = load(proj_hbm.at[span], proj.at[span], 1 + slot)
    later_loads = [
        load(source, target, 7 + slot)
        for slot, (source, target) in enumerate(
            (
                (grad_hbm, grad), (filt_hbm, filt), (spread_hbm, spread), (cos_hbm, cos_twist),
                (sin_hbm, sin_twist), (mix_hbm, mix), (gather_hbm, gather),
            )
        )
    ]

    gate = pltpu.get_barrier_semaphore()
    for step in range(1, 16):
        signal(gate, high * 16 + (low + step) % 16)
    for step in range(1, 16):
        signal(gate, ((high + step) % 16) * 16 + low)
    signal(gate, after)
    signal(gate, before)

    row = lax.broadcasted_iota(jnp.int32, (A, 128), 0)
    lane = lax.broadcasted_iota(jnp.int32, (A, 128), 1)
    for lag in range(1, TAPS):
        span = slice((lag - 1) * 128, lag * 128)
        shift[0, :, span] = (row == lane + 128 - lag).astype(F32).astype(BF16)
    last = one_hot((16, A), A - TAPS + 1, TAPS - 1)
    first = one_hot((16, A), 0, TAPS - 1)
    ahead = one_hot((16, 128), 128 - TAPS + 1, TAPS - 1)
    behind = one_hot((16, 128), 0, TAPS - 1)

    def take_edge(part, turn):
        parts[part, turn].wait()
        span = pl.ds(channels(part, turn), BLOCK)
        edge_out[0, :, span] = lax.dot_general(last, proj[span, :], NT, preferred_element_type=F32).astype(BF16)

    for part, turn in ((1, 0), (2, 0), (1, 1), (2, 1)):
        take_edge(part, turn)
    pl.semaphore_wait(gate, 32)
    tail = pl.ds(CH, 2 * CH)
    edge_kv = remote(edge_out.at[0, :, tail], edge_in.at[0, :, tail], sem_first, after)
    edge_kv.start()
    for step in range(1, 16):
        signal(rounds.at[0], ((high + step) % 16) * 16 + low)

    taps_load.wait()
    padded[...] = jnp.zeros_like(padded)
    padded[:TAPS, :] = taps[...].astype(F32)
    for block in range(0, 3 * CH, 128):
        weights[block : block + 128, :] = jnp.transpose(padded[:, block : block + 128])

    def filtered(part, turn, half):
        span = pl.ds(channels(part, turn), BLOCK)
        if half == 0:
            prior = lax.dot_general(edge_in[0, :, span], ahead, TN, preferred_element_type=F32).astype(BF16)
            prior = jnp.where(me > 0, prior, jnp.zeros_like(prior))
            window = jnp.concatenate([prior, proj[span, :128]], axis=1)
        else:
            window = proj[span, :]
        scale = weights[span, :]
        lanes = slice(half * 128, half * 128 + 128)
        moved = dot(window, shift[0])
        total = scale[:, 0:1] * proj[span, lanes].astype(F32)
        for lag in range(1, TAPS):
            total = total + scale[:, lag : lag + 1] * moved[:, (lag - 1) * 128 : lag * 128]
        total = total.astype(BF16)
        feat[span, lanes] = total
        return total.astype(F32)

    def chips(turn):
        return pl.ds(pl.multiple_of(channels(0, turn) // 8, SIDE), SIDE)

    def make_product(turn, half):
        keys = filtered(1, turn, half)
        values = filtered(2, turn, half)
        both = (keys * values).reshape(SIDE, 8, 128)
        prod[chips(turn), :, half * 128 : half * 128 + 128] = both.astype(BF16)

    def make_cotangent(turn, half):
        queries = filtered(0, turn, half)
        lanes = slice(half * 128, half * 128 + 128)
        both = (queries * grad[pl.ds(channels(0, turn), BLOCK), lanes].astype(F32)).reshape(SIDE, 8, 128)
        cotp[chips(turn), :, lanes] = both.astype(BF16)

    def send_side(source, target, sems, turn):
        base = (side * (1 - turn) + (1 - side) * turn) * SIDE

        def send(step, carry):
            other = base + (within + step) % SIDE
            remote(source.at[other], target.at[chip], sems.at[turn], other * 2 + core).start()
            return carry

        lax.fori_loop(1 - turn, SIDE, send, 0)

    def keep_own(source, target, slot):
        keep = pltpu.make_async_copy(source.at[chip], target.at[chip], own.at[slot])
        keep.start()
        return keep

    def settle_send(source, target, sems, turn):
        some = pl.ds(0, SIDE - 1 + turn)
        remote(source.at[some], target.at[some], sems.at[turn], ((chip + 1) % CHIPS) * 2 + core).wait_send()

    def settle_recv(source, target, sems, turn):
        some = pl.ds(0, SIDE - 1 + turn)
        remote(source.at[some], target.at[some], sems.at[turn], ((chip + 1) % CHIPS) * 2 + core).wait_recv()

    make_product(0, 1)
    edge_kv.wait()
    make_product(0, 0)
    pl.semaphore_wait(rounds.at[0], 15)
    send_side(prod, recv_p, sem_p, 0)
    keep_p = keep_own(prod, recv_p, 0)
    make_product(1, 1)
    make_product(1, 0)
    send_side(prod, recv_p, sem_p, 1)
    take_edge(0, 0)
    take_edge(0, 1)
    head = pl.ds(0, CH)
    edge_query = remote(edge_out.at[0, :, head], edge_in.at[0, :, head], sem_edge, after)
    edge_query.start()
    later_loads[0].wait()
    make_cotangent(0, 1)
    edge_query.wait()
    make_cotangent(0, 0)
    send_side(cotp, recv_g, sem_g, 0)
    keep_g = keep_own(cotp, recv_g, 1)
    make_cotangent(1, 1)
    make_cotangent(1, 0)
    send_side(cotp, recv_g, sem_g, 1)

    for copy in later_loads[1:]:
        copy.wait()
    mixback[:A, :A] = mix[:A, :A]
    mixback[A:, A:] = mix[A:, A:]
    mixback[:A, A:] = mix[A:, :A]
    mixback[A:, :A] = mix[:A, A:]
    for lag in range(1, TAPS):
        span = slice((lag - 1) * 128, lag * 128)
        shift[1, :, span] = (row == lane + lag).astype(F32).astype(BF16)

    def forward(signal_rows):
        raw = dot(spread[...], signal_rows)
        re, im, odd = raw[:HALF], raw[HALF : 2 * HALF], raw[2 * HALF :]
        ct, st = cos_twist[:HALF, :], sin_twist[:HALF, :]
        bins[:HALF, :A] = (re * ct + im * st).astype(BF16)
        bins[:HALF, A:] = (im * ct - re * st).astype(BF16)
        bins[HALF:, :A] = (odd * cos_twist[HALF:, :]).astype(BF16)
        bins[HALF:, A:] = (-odd * sin_twist[HALF:, :]).astype(BF16)
        return dot(bins[...], mix[...])

    def inverse(re, im):
        bins[:, :A] = re.astype(BF16)
        bins[:, A:] = im.astype(BF16)
        back = dot(bins[...], mixback[...])
        re, im = back[:, :A], back[:, A:]
        ct, st = cos_twist[...], sin_twist[...]
        turn_re = re * ct - im * st
        turn_im = im[:HALF] * ct[:HALF] + re[:HALF] * st[:HALF]
        top = lax.broadcasted_iota(jnp.int32, (16, A), 0) == 0
        rows[:HALF, :] = turn_re[:HALF].astype(BF16)
        rows[HALF:, :] = turn_im.astype(BF16)
        rows[HALF : HALF + 16, :] = jnp.where(top, turn_re[HALF:], turn_im[:16]).astype(BF16)
        return dot(gather[...], rows[...]) * (1.0 / PAD)

    def spread_filter(step, carry):
        piece = filt[:, pl.ds(pl.multiple_of(step * 1024, 1024), 1024)].astype(F32)
        fold[0, pl.ds(pl.multiple_of(step * 8, 8), 8), :] = piece.reshape(8, 128)
        return carry

    lax.fori_loop(0, SEQ // 1024, spread_filter, 0)
    for parity in range(2):
        for half in range(2):
            rows[parity * CHIPS : (parity + 1) * CHIPS, half * 128 : half * 128 + 128] = fold[
                0, pl.ds(2 * parity + half, CHIPS, stride=4), :
            ].astype(BF16)
    fspec[...] = forward(rows[:HALF, :])

    def swap_here(stream, channel, sems):
        return remote(
            swap_out.at[stream, channel], signals.at[stream * CPG + channel, mine, :], sems.at[channel], twin
        )

    def swap_back(stream, channel, sems):
        return remote(swap_out.at[2 + stream, channel], swap_in.at[stream, channel], sems.at[channel], twin)

    def unfold(received, stream, sems):
        for half in range(2):
            lanes = slice(half * 128, half * 128 + 128)
            fold[half] = received[:, :, lanes].astype(F32).reshape(CHIPS * 8, 128)
        for channel in range(CPG):
            for half in range(2):
                lanes = slice(half * 128, half * 128 + 128)
                low_set = fold[half, pl.ds(channel, CHIPS, stride=8), :]
                high_set = fold[half, pl.ds(CPG + channel, CHIPS, stride=8), :]
                signals[stream * CPG + channel, mine, lanes] = jnp.where(core == 0, low_set, high_set).astype(BF16)
                swap_out[stream, channel, :, lanes] = jnp.where(core == 0, high_set, low_set).astype(BF16)
            swap_here(stream, channel, sems).start()

    def refold(stream, ready, sems):
        for channel in range(CPG):
            swap_back(stream, channel, sems).wait()
            for half in range(2):
                lanes = slice(half * 128, half * 128 + 128)
                here = kept[stream, channel, :, lanes].astype(F32)
                there = swap_in[stream, channel, :, lanes].astype(F32)
                fold[half, pl.ds(channel, CHIPS, stride=8), :] = jnp.where(core == 0, here, there)
                fold[half, pl.ds(CPG + channel, CHIPS, stride=8), :] = jnp.where(core == 0, there, here)
        for half in range(2):
            ready[:, :, half * 128 : half * 128 + 128] = fold[half].reshape(CHIPS, 8, 128).astype(BF16)

    def put_away(result, stream, channel, sems):
        even, odd = result[:CHIPS], result[CHIPS:]
        kept[stream, channel] = jnp.where(core == 0, even, odd).astype(BF16)
        swap_out[2 + stream, channel] = jnp.where(core == 0, odd, even).astype(BF16)
        swap_back(stream, channel, sems).start()

    keep_p.wait()
    for turn in range(2):
        settle_recv(prod, recv_p, sem_p, turn)
    unfold(recv_p, 0, swap_p)

    def convolve(channel, carry):
        swap_here(0, channel, swap_p).wait()
        spec = forward(signals[channel])
        kspec[channel] = spec
        re, im = spec[:, :A], spec[:, A:]
        f_re, f_im = fspec[:, :A], fspec[:, A:]
        result = inverse((f_re * re - f_im * im) * SCALE, (f_re * im + f_im * re) * SCALE)
        put_away(result, 0, channel, swap_c)
        return carry

    lax.fori_loop(0, CPG, convolve, 0)
    refold(0, ready_c, swap_c)
    for turn in range(2):
        send_side(ready_c, tok_c, sem_c, turn)
    keep_c = keep_own(ready_c, tok_c, 2)

    keep_g.wait()
    for turn in range(2):
        settle_recv(cotp, recv_g, sem_g, turn)
    unfold(recv_g, 1, swap_g)
    cross[...] = jnp.zeros_like(cross)

    def correlate(channel, carry):
        swap_here(1, channel, swap_g).wait()
        spec = forward(signals[CPG + channel])
        re, im = spec[:, :A], spec[:, A:]
        k_re, k_im = kspec[channel, :, :A], kspec[channel, :, A:]
        cross[:, :A] = cross[:, :A] + (k_re * re + k_im * im)
        cross[:, A:] = cross[:, A:] + (k_re * im - k_im * re)
        f_re, f_im = fspec[:, :A], fspec[:, A:]
        result = inverse((f_re * re + f_im * im) * SCALE, (f_re * im - f_im * re) * SCALE)
        put_away(result, 1, channel, swap_b)
        return carry

    lax.fori_loop(0, CPG, correlate, 0)
    refold(1, ready_b, swap_b)
    for turn in range(2):
        send_side(ready_b, tok_b, sem_b, turn)
    keep_b = keep_own(ready_b, tok_b, 3)

    result = inverse(cross[:, :A], cross[:, A:]) * SCALE
    for parity in range(2):
        for half in range(2):
            fgrad[pl.ds(2 * parity + half, CHIPS, stride=4), :] = result[
                parity * CHIPS : (parity + 1) * CHIPS, half * 128 : half * 128 + 128
            ]

    keep_c.wait()
    for turn in range(2):
        settle_recv(ready_c, tok_c, sem_c, turn)

    def use_conv(step, carry):
        span = pl.ds(pl.multiple_of(step * BLOCK, BLOCK), BLOCK)
        conv = tok_c[pl.ds(step * SIDE, SIDE)].astype(F32).reshape(BLOCK, A)
        mixed[span, :] = (feat[span, :].astype(F32) * conv).astype(BF16)
        back = (grad[span, :].astype(F32) * conv).astype(BF16)
        dfeat[span, :] = back
        edge_q[0, :, span] = lax.dot_general(first, back, NT, preferred_element_type=F32).astype(BF16)
        return carry

    lax.fori_loop(0, CH // BLOCK, use_conv, 0)
    edge_back = remote(edge_q.at[0], edge_q.at[1], sem_edge_q, before)
    edge_back.start()

    def gathered(start, half, halo):
        span = pl.ds(pl.multiple_of(start, BLOCK), BLOCK)
        lanes = slice(half * 128, half * 128 + 128)
        if half == 0:
            window = dfeat[span, :]
        else:
            later = lax.dot_general(halo, behind, TN, preferred_element_type=F32).astype(BF16)
            later = jnp.where(me < DEVICES - 1, later, jnp.zeros_like(later))
            window = jnp.concatenate([dfeat[span, 128:], later], axis=1)
        scale = weights[span, :]
        moved = dot(window, shift[1])
        total = scale[:, 0:1] * dfeat[span, lanes].astype(F32)
        for lag in range(1, TAPS):
            total = total + scale[:, lag : lag + 1] * moved[:, (lag - 1) * 128 : lag * 128]
        pgrad[span, lanes] = total.astype(BF16)

    for step in range(CH // BLOCK):
        gathered(step * BLOCK, 0, None)
    edge_back.wait()
    for step in range(CH // BLOCK):
        gathered(step * BLOCK, 1, edge_q[1, :, step * BLOCK : (step + 1) * BLOCK])

    def use_back(turn, sems):
        back = tok_b[chips(turn)].astype(F32).reshape(BLOCK, A)
        for part, other in ((1, 2), (2, 1)):
            result = (feat[pl.ds(channels(other, turn), BLOCK), :].astype(F32) * back).astype(BF16)
            target = pl.ds(channels(part, turn), BLOCK)
            dfeat[target, :] = result
            edge_out[1, :, target] = lax.dot_general(first, result, NT, preferred_element_type=F32).astype(BF16)
        edges = []
        for part in (1, 2):
            target = pl.ds(channels(part, turn), BLOCK)
            edge = remote(edge_out.at[1, :, target], edge_in.at[1, :, target], sems.at[part - 1], before)
            edge.start()
            edges.append(edge)
        return edges

    keep_b.wait()
    settle_recv(ready_b, tok_b, sem_b, 0)
    edges = use_back(0, sem_edge_own)
    for part in (1, 2):
        gathered(channels(part, 0), 0, None)
    settle_recv(ready_b, tok_b, sem_b, 1)
    edges += use_back(1, sem_edge_rest)
    for part in (1, 2):
        gathered(channels(part, 1), 0, None)
    for source, target, sems in ((prod, recv_p, sem_p), (cotp, recv_g, sem_g), (ready_c, tok_c, sem_c), (ready_b, tok_b, sem_b)):
        for turn in range(2):
            settle_send(source, target, sems, turn)
    for edge in edges:
        edge.wait()
    for turn in range(2):
        for part in (1, 2):
            gathered(channels(part, turn), 1, edge_in[1, :, pl.ds(channels(part, turn), BLOCK)])


def shards(projections, short_filter, long_filter, out_grad):
    vmem = pl.BlockSpec(memory_space=pltpu.VMEM)
    hbm = pl.BlockSpec(memory_space=pltpu.HBM)
    tokens = pltpu.VMEM((CHIPS, 8, A), BF16)
    pair = pltpu.SemaphoreType.DMA((2,))
    sides = pltpu.SemaphoreType.DMA((2, 2))
    swaps = pltpu.SemaphoreType.DMA((CPG, 2))
    operands = (projections, short_filter, long_filter, out_grad, *make_tables())
    mixed, proj_grad, filter_grad = pl.pallas_call(
        mixer_kernel,
        out_shape=(
            jax.ShapeDtypeStruct((CH, A), BF16),
            jax.ShapeDtypeStruct((3 * CH, A), BF16),
            jax.ShapeDtypeStruct((SEQ // 128, 128), F32),
        ),
        in_specs=[hbm] * 9,
        out_specs=(vmem, vmem, vmem),
        scratch_shapes=[
            *[pltpu.VMEM(operand.shape, operand.dtype) for operand in operands],
            pltpu.VMEM((8, 3 * CH), F32),
            pltpu.VMEM((3 * CH, 8), F32),
            pltpu.VMEM((2, A, 128 * (TAPS - 1)), BF16),
            pltpu.VMEM((3 * CH, A), BF16),
            tokens, tokens, tokens, tokens,
            pltpu.VMEM((2, CHIPS * 8, 128), F32),
            pltpu.VMEM((2 * CPG, HALF, A), BF16),
            pltpu.VMEM((4, CPG, CHIPS, A), BF16),
            pltpu.VMEM((2, CPG, CHIPS, A), BF16),
            pltpu.VMEM((2, CPG, CHIPS, A), BF16),
            tokens, tokens, tokens, tokens,
            pltpu.VMEM((ROWS, 2 * A), F32),
            pltpu.VMEM((CPG, ROWS, 2 * A), F32),
            pltpu.VMEM((ROWS, 2 * A), F32),
            pltpu.VMEM((ROWS, 2 * A), BF16),
            pltpu.VMEM((2 * HALF, A), BF16),
            pltpu.VMEM((2 * A, 2 * A), BF16),
            pltpu.VMEM((3 * CH, A), BF16),
            pltpu.VMEM((2, 16, 3 * CH), BF16),
            pltpu.VMEM((2, 16, 3 * CH), BF16),
            pltpu.VMEM((2, 16, CH), BF16),
            pltpu.SemaphoreType.REGULAR((1,)),
            pltpu.SemaphoreType.DMA((14,)),
            pair, pair, sides, sides, pair, sides, sides, sides, sides,
            swaps, swaps, swaps, swaps,
            pltpu.SemaphoreType.DMA((4,)),
        ],
        compiler_params=pltpu.CompilerParams(collective_id=0, has_side_effects=True, vmem_limit_bytes=44 << 20),
        name="mixer",
    )(*[pltpu.with_memory_space_constraint(operand, pltpu.HBM) for operand in operands])
    return (mixed, proj_grad, filter_grad.reshape(1, SEQ))


def solution(mesh):
    placed = (P(None, ("dp", "ctx")), P(), P(("dp", "ctx"), None), P(None, ("dp", "ctx")))
    return jax.shard_map(
        shards,
        mesh=mesh,
        in_specs=placed,
        out_specs=(P(None, ("dp", "ctx")), P(None, ("dp", "ctx")), P(("dp", "ctx"), None)),
        check_vma=False,
    )
```

```python
import functools
import math

import jax
import jax.numpy as jnp
import numpy as np
from jax import lax
from jax.experimental import pallas as pl
from jax.experimental.pallas import tpu as pltpu
from jax.sharding import PartitionSpec as P

CPG = 4
TAPS = 7
LANES = 32
CH = 1024
SEQ = 65536
PAD = 2 * SEQ
A = 256
B = 512
HALF = 256
ROWS = 272
CHIPS = 128
DEVICES = 256
SCALE = SEQ ** -0.5
BLOCK = 512
SIDE = 64
NT = (((1,), (1,)), ((), ()))
TN = (((0,), (0,)), ((), ()))
F32 = jnp.float32
BF16 = jnp.bfloat16


def make_tables():
    order = np.concatenate([np.arange(0, HALF, 2), np.arange(1, HALF, 2)])
    d = np.arange(HALF)[:, None]
    outer = 2 * np.pi * ((d * order[None, :]) % B) / B
    cos_outer, sin_outer = np.cos(outer), np.sin(outer)
    sign = 1.0 - 2.0 * (order % 2)
    spread = np.zeros((2 * HALF + 16, HALF))
    spread[:HALF] = cos_outer
    spread[HALF : 2 * HALF] = -sin_outer
    spread[2 * HALF] = sign
    gather = np.zeros((HALF, 2 * HALF))
    gather[:, :HALF] = 2 * cos_outer.T
    gather[:, 0] = 1.0
    gather[:, HALF:] = -2 * sin_outer.T
    gather[:, HALF] = sign
    e = np.arange(A)
    inner = 2 * np.pi * ((e[:, None] * e[None, :]) % A) / A
    cos_inner, sin_inner = np.cos(inner), np.sin(inner)
    mix = np.block([[cos_inner, -sin_inner], [sin_inner, cos_inner]])
    twist = 2 * np.pi * (np.arange(ROWS)[:, None] * e[None, :]) / PAD
    return (
        jnp.asarray(spread.astype(np.float32), BF16),
        jnp.asarray(gather.astype(np.float32), BF16),
        jnp.asarray(mix.astype(np.float32), BF16),
        jnp.asarray(np.cos(twist).astype(np.float32)),
        jnp.asarray(np.sin(twist).astype(np.float32)),
    )


def place(index):
    return (index // LANES, index % LANES)


def signal(sem, index):
    pl.semaphore_signal(sem, inc=1, device_id=place(index), device_id_type=pl.DeviceIdType.MESH)


def remote(source, target, sems, index):
    return pltpu.make_async_remote_copy(
        source, target, sems.at[0], sems.at[1], device_id=place(index), device_id_type=pl.DeviceIdType.MESH
    )


def dot(first, second):
    return jnp.dot(first, second, preferred_element_type=F32)


def one_hot(shape, offset, limit):
    row = lax.broadcasted_iota(jnp.int32, shape, 0)
    lane = lax.broadcasted_iota(jnp.int32, shape, 1)
    return ((lane == row + offset) & (row < limit)).astype(F32).astype(BF16)


def mixer_kernel(
    proj_hbm, taps_hbm, filt_hbm, grad_hbm, spread_hbm, gather_hbm, mix_hbm, cos_hbm, sin_hbm,
    mixed, pgrad, fgrad,
    proj, taps, filt, grad, spread, gather, mix, cos_twist, sin_twist, padded,
    weights, shift, feat, prod, cotp, recv_p, recv_g, fold, signals, swap_out, swap_in, kept, ready_c, ready_b, tok_c, tok_b,
    fspec, kspec, cross, bins, rows, mixback, dfeat, edge_out, edge_in, edge_q,
    rounds, loads, sem_edge, sem_edge_q, sem_edge_own, sem_edge_rest, sem_first, sem_p, sem_g, sem_c, sem_b,
    swap_p, swap_g, swap_c, swap_b, own,
):
    me = lax.axis_index("dp") * LANES + lax.axis_index("ctx")
    chip, core = me // 2, me % 2
    high, low = me // 16, me % 16
    side, within = chip // SIDE, chip % SIDE
    twin = chip * 2 + 1 - core
    after, before = (me + 1) % DEVICES, (me + DEVICES - 1) % DEVICES
    mine = pl.ds(pl.multiple_of(core * CHIPS, CHIPS), CHIPS)

    def channels(part, turn):
        return pl.multiple_of(part * CH + (side * (1 - turn) + (1 - side) * turn) * BLOCK, BLOCK)

    def load(source, target, slot):
        copy = pltpu.make_async_copy(source, target, loads.at[slot])
        copy.start()
        return copy

    taps_load = load(taps_hbm, taps, 0)
    parts = {}
    for slot, (part, turn) in enumerate(((1, 0), (2, 0), (1, 1), (2, 1), (0, 0), (0, 1))):
        span = pl.ds(channels(part, turn), BLOCK)
        parts[part, turn] = load(proj_hbm.at[span], proj.at[span], 1 + slot)
    gate = pltpu.get_barrier_semaphore()
    for step in range(1, 16):
        signal(gate, high * 16 + (low + step) % 16)
    for step in range(1, 16):
        signal(gate, ((high + step) % 16) * 16 + low)
    signal(gate, after)
    signal(gate, before)

    later_loads = [
        load(source, target, 7 + slot)
        for slot, (source, target) in enumerate(
            (
                (grad_hbm, grad), (filt_hbm, filt), (spread_hbm, spread), (cos_hbm, cos_twist),
                (sin_hbm, sin_twist), (mix_hbm, mix), (gather_hbm, gather),
            )
        )
    ]

    row = lax.broadcasted_iota(jnp.int32, (A, 128), 0)
    lane = lax.broadcasted_iota(jnp.int32, (A, 128), 1)
    for lag in range(1, TAPS):
        span = slice((lag - 1) * 128, lag * 128)
        shift[0, :, span] = (row == lane + 128 - lag).astype(F32).astype(BF16)
    last = one_hot((16, A), A - TAPS + 1, TAPS - 1)
    first = one_hot((16, A), 0, TAPS - 1)
    ahead = one_hot((16, 128), 128 - TAPS + 1, TAPS - 1)
    behind = one_hot((16, 128), 0, TAPS - 1)

    taps_load.wait()
    padded[...] = jnp.zeros_like(padded)
    padded[:TAPS, :] = taps[...].astype(F32)
    for block in range(0, 3 * CH, 128):
        weights[block : block + 128, :] = jnp.transpose(padded[:, block : block + 128])

    def take_edge(part, turn):
        parts[part, turn].wait()
        span = pl.ds(channels(part, turn), BLOCK)
        edge_out[0, :, span] = lax.dot_general(last, proj[span, :], NT, preferred_element_type=F32).astype(BF16)

    for part, turn in ((1, 0), (2, 0), (1, 1), (2, 1)):
        take_edge(part, turn)
    pl.semaphore_wait(gate, 32)
    tail = pl.ds(CH, 2 * CH)
    edge_kv = remote(edge_out.at[0, :, tail], edge_in.at[0, :, tail], sem_first, after)
    edge_kv.start()
    for step in range(1, 16):
        signal(rounds.at[0], ((high + step) % 16) * 16 + low)

    def filtered(part, turn, half):
        span = pl.ds(channels(part, turn), BLOCK)
        if half == 0:
            prior = lax.dot_general(edge_in[0, :, span], ahead, TN, preferred_element_type=F32).astype(BF16)
            prior = jnp.where(me > 0, prior, jnp.zeros_like(prior))
            window = jnp.concatenate([prior, proj[span, :128]], axis=1)
        else:
            window = proj[span, :]
        scale = weights[span, :]
        lanes = slice(half * 128, half * 128 + 128)
        moved = dot(window, shift[0])
        total = scale[:, 0:1] * proj[span, lanes].astype(F32)
        for lag in range(1, TAPS):
            total = total + scale[:, lag : lag + 1] * moved[:, (lag - 1) * 128 : lag * 128]
        total = total.astype(BF16)
        feat[span, lanes] = total
        return total.astype(F32)

    def chips(turn):
        return pl.ds(pl.multiple_of(channels(0, turn) // 8, SIDE), SIDE)

    def make_product(turn, half):
        keys = filtered(1, turn, half)
        values = filtered(2, turn, half)
        both = (keys * values).reshape(SIDE, 8, 128)
        prod[chips(turn), :, half * 128 : half * 128 + 128] = both.astype(BF16)

    def make_cotangent(turn, half):
        queries = filtered(0, turn, half)
        lanes = slice(half * 128, half * 128 + 128)
        both = (queries * grad[pl.ds(channels(0, turn), BLOCK), lanes].astype(F32)).reshape(SIDE, 8, 128)
        cotp[chips(turn), :, lanes] = both.astype(BF16)

    def send_side(source, target, sems, turn):
        base = (side * (1 - turn) + (1 - side) * turn) * SIDE

        def send(step, carry):
            other = base + (within + step) % SIDE
            remote(source.at[other], target.at[chip], sems.at[turn], other * 2 + core).start()
            return carry

        lax.fori_loop(1 - turn, SIDE, send, 0)

    def keep_own(source, target, slot):
        keep = pltpu.make_async_copy(source.at[chip], target.at[chip], own.at[slot])
        keep.start()
        return keep

    def settle_send(source, target, sems, turn):
        some = pl.ds(0, SIDE - 1 + turn)
        remote(source.at[some], target.at[some], sems.at[turn], ((chip + 1) % CHIPS) * 2 + core).wait_send()

    def settle_recv(source, target, sems, turn):
        some = pl.ds(0, SIDE - 1 + turn)
        remote(source.at[some], target.at[some], sems.at[turn], ((chip + 1) % CHIPS) * 2 + core).wait_recv()

    make_product(0, 1)
    edge_kv.wait()
    make_product(0, 0)
    pl.semaphore_wait(rounds.at[0], 15)
    send_side(prod, recv_p, sem_p, 0)
    keep_p = keep_own(prod, recv_p, 0)
    make_product(1, 1)
    make_product(1, 0)
    send_side(prod, recv_p, sem_p, 1)
    take_edge(0, 0)
    take_edge(0, 1)
    head = pl.ds(0, CH)
    edge_query = remote(edge_out.at[0, :, head], edge_in.at[0, :, head], sem_edge, after)
    edge_query.start()
    later_loads[0].wait()
    make_cotangent(0, 1)
    edge_query.wait()
    make_cotangent(0, 0)
    send_side(cotp, recv_g, sem_g, 0)
    keep_g = keep_own(cotp, recv_g, 1)
    make_cotangent(1, 1)
    make_cotangent(1, 0)
    send_side(cotp, recv_g, sem_g, 1)

    for copy in later_loads[1:]:
        copy.wait()
    mixback[:A, :A] = mix[:A, :A]
    mixback[A:, A:] = mix[A:, A:]
    mixback[:A, A:] = mix[A:, :A]
    mixback[A:, :A] = mix[:A, A:]
    for lag in range(1, TAPS):
        span = slice((lag - 1) * 128, lag * 128)
        shift[1, :, span] = (row == lane + lag).astype(F32).astype(BF16)

    def forward(signal_rows):
        raw = dot(spread[...], signal_rows)
        re, im, odd = raw[:HALF], raw[HALF : 2 * HALF], raw[2 * HALF :]
        ct, st = cos_twist[:HALF, :], sin_twist[:HALF, :]
        bins[:HALF, :A] = (re * ct + im * st).astype(BF16)
        bins[:HALF, A:] = (im * ct - re * st).astype(BF16)
        bins[HALF:, :A] = (odd * cos_twist[HALF:, :]).astype(BF16)
        bins[HALF:, A:] = (-odd * sin_twist[HALF:, :]).astype(BF16)
        return dot(bins[...], mix[...])

    def inverse(re, im):
        bins[:, :A] = re.astype(BF16)
        bins[:, A:] = im.astype(BF16)
        back = dot(bins[...], mixback[...])
        re, im = back[:, :A], back[:, A:]
        ct, st = cos_twist[...], sin_twist[...]
        turn_re = re * ct - im * st
        turn_im = im[:HALF] * ct[:HALF] + re[:HALF] * st[:HALF]
        top = lax.broadcasted_iota(jnp.int32, (16, A), 0) == 0
        rows[:HALF, :] = turn_re[:HALF].astype(BF16)
        rows[HALF:, :] = turn_im.astype(BF16)
        rows[HALF : HALF + 16, :] = jnp.where(top, turn_re[HALF:], turn_im[:16]).astype(BF16)
        return dot(gather[...], rows[...]) * (1.0 / PAD)

    def spread_filter(step, carry):
        piece = filt[:, pl.ds(pl.multiple_of(step * 1024, 1024), 1024)].astype(F32)
        fold[0, pl.ds(pl.multiple_of(step * 8, 8), 8), :] = piece.reshape(8, 128)
        return carry

    lax.fori_loop(0, SEQ // 1024, spread_filter, 0)
    for parity in range(2):
        for half in range(2):
            rows[parity * CHIPS : (parity + 1) * CHIPS, half * 128 : half * 128 + 128] = fold[
                0, pl.ds(2 * parity + half, CHIPS, stride=4), :
            ].astype(BF16)
    fspec[...] = forward(rows[:HALF, :])

    def swap_here(stream, channel, sems):
        return remote(
            swap_out.at[stream, channel], signals.at[stream * CPG + channel, mine, :], sems.at[channel], twin
        )

    def swap_back(stream, channel, sems):
        return remote(swap_out.at[2 + stream, channel], swap_in.at[stream, channel], sems.at[channel], twin)

    def unfold(received, stream, sems):
        for half in range(2):
            lanes = slice(half * 128, half * 128 + 128)
            fold[half] = received[:, :, lanes].astype(F32).reshape(CHIPS * 8, 128)
        for channel in range(CPG):
            for half in range(2):
                lanes = slice(half * 128, half * 128 + 128)
                low_set = fold[half, pl.ds(channel, CHIPS, stride=8), :]
                high_set = fold[half, pl.ds(CPG + channel, CHIPS, stride=8), :]
                signals[stream * CPG + channel, mine, lanes] = jnp.where(core == 0, low_set, high_set).astype(BF16)
                swap_out[stream, channel, :, lanes] = jnp.where(core == 0, high_set, low_set).astype(BF16)
            swap_here(stream, channel, sems).start()

    def refold(stream, ready, sems):
        for channel in range(CPG):
            swap_back(stream, channel, sems).wait()
            for half in range(2):
                lanes = slice(half * 128, half * 128 + 128)
                here = kept[stream, channel, :, lanes].astype(F32)
                there = swap_in[stream, channel, :, lanes].astype(F32)
                fold[half, pl.ds(channel, CHIPS, stride=8), :] = jnp.where(core == 0, here, there)
                fold[half, pl.ds(CPG + channel, CHIPS, stride=8), :] = jnp.where(core == 0, there, here)
        for half in range(2):
            ready[:, :, half * 128 : half * 128 + 128] = fold[half].reshape(CHIPS, 8, 128).astype(BF16)

    def put_away(result, stream, channel, sems):
        even, odd = result[:CHIPS], result[CHIPS:]
        kept[stream, channel] = jnp.where(core == 0, even, odd).astype(BF16)
        swap_out[2 + stream, channel] = jnp.where(core == 0, odd, even).astype(BF16)
        swap_back(stream, channel, sems).start()

    keep_p.wait()
    for turn in range(2):
        settle_recv(prod, recv_p, sem_p, turn)
    unfold(recv_p, 0, swap_p)

    def convolve(channel, carry):
        swap_here(0, channel, swap_p).wait()
        spec = forward(signals[channel])
        kspec[channel] = spec
        re, im = spec[:, :A], spec[:, A:]
        f_re, f_im = fspec[:, :A], fspec[:, A:]
        result = inverse((f_re * re - f_im * im) * SCALE, (f_re * im + f_im * re) * SCALE)
        put_away(result, 0, channel, swap_c)
        return carry

    lax.fori_loop(0, CPG, convolve, 0)
    refold(0, ready_c, swap_c)
    for turn in range(2):
        send_side(ready_c, tok_c, sem_c, turn)
    keep_c = keep_own(ready_c, tok_c, 2)

    keep_g.wait()
    for turn in range(2):
        settle_recv(cotp, recv_g, sem_g, turn)
    unfold(recv_g, 1, swap_g)
    cross[...] = jnp.zeros_like(cross)

    def correlate(channel, carry):
        swap_here(1, channel, swap_g).wait()
        spec = forward(signals[CPG + channel])
        re, im = spec[:, :A], spec[:, A:]
        k_re, k_im = kspec[channel, :, :A], kspec[channel, :, A:]
        cross[:, :A] = cross[:, :A] + (k_re * re + k_im * im)
        cross[:, A:] = cross[:, A:] + (k_re * im - k_im * re)
        f_re, f_im = fspec[:, :A], fspec[:, A:]
        result = inverse((f_re * re + f_im * im) * SCALE, (f_re * im - f_im * re) * SCALE)
        put_away(result, 1, channel, swap_b)
        return carry

    lax.fori_loop(0, CPG, correlate, 0)
    refold(1, ready_b, swap_b)
    for turn in range(2):
        send_side(ready_b, tok_b, sem_b, turn)
    keep_b = keep_own(ready_b, tok_b, 3)

    result = inverse(cross[:, :A], cross[:, A:]) * SCALE
    for parity in range(2):
        for half in range(2):
            fgrad[pl.ds(2 * parity + half, CHIPS, stride=4), :] = result[
                parity * CHIPS : (parity + 1) * CHIPS, half * 128 : half * 128 + 128
            ]

    keep_c.wait()
    for turn in range(2):
        settle_recv(ready_c, tok_c, sem_c, turn)

    def use_conv(step, carry):
        span = pl.ds(pl.multiple_of(step * BLOCK, BLOCK), BLOCK)
        conv = tok_c[pl.ds(step * SIDE, SIDE)].astype(F32).reshape(BLOCK, A)
        mixed[span, :] = (feat[span, :].astype(F32) * conv).astype(BF16)
        back = (grad[span, :].astype(F32) * conv).astype(BF16)
        dfeat[span, :] = back
        edge_q[0, :, span] = lax.dot_general(first, back, NT, preferred_element_type=F32).astype(BF16)
        return carry

    lax.fori_loop(0, CH // BLOCK, use_conv, 0)
    edge_back = remote(edge_q.at[0], edge_q.at[1], sem_edge_q, before)
    edge_back.start()

    def gathered(start, half, halo):
        span = pl.ds(pl.multiple_of(start, BLOCK), BLOCK)
        lanes = slice(half * 128, half * 128 + 128)
        if half == 0:
            window = dfeat[span, :]
        else:
            later = lax.dot_general(halo, behind, TN, preferred_element_type=F32).astype(BF16)
            later = jnp.where(me < DEVICES - 1, later, jnp.zeros_like(later))
            window = jnp.concatenate([dfeat[span, 128:], later], axis=1)
        scale = weights[span, :]
        moved = dot(window, shift[1])
        total = scale[:, 0:1] * dfeat[span, lanes].astype(F32)
        for lag in range(1, TAPS):
            total = total + scale[:, lag : lag + 1] * moved[:, (lag - 1) * 128 : lag * 128]
        pgrad[span, lanes] = total.astype(BF16)

    for step in range(CH // BLOCK):
        gathered(step * BLOCK, 0, None)
    edge_back.wait()
    for step in range(CH // BLOCK):
        gathered(step * BLOCK, 1, edge_q[1, :, step * BLOCK : (step + 1) * BLOCK])

    def use_back(turn, sems):
        back = tok_b[chips(turn)].astype(F32).reshape(BLOCK, A)
        for part, other in ((1, 2), (2, 1)):
            result = (feat[pl.ds(channels(other, turn), BLOCK), :].astype(F32) * back).astype(BF16)
            target = pl.ds(channels(part, turn), BLOCK)
            dfeat[target, :] = result
            edge_out[1, :, target] = lax.dot_general(first, result, NT, preferred_element_type=F32).astype(BF16)
        edges = []
        for part in (1, 2):
            target = pl.ds(channels(part, turn), BLOCK)
            edge = remote(edge_out.at[1, :, target], edge_in.at[1, :, target], sems.at[part - 1], before)
            edge.start()
            edges.append(edge)
        return edges

    keep_b.wait()
    settle_recv(ready_b, tok_b, sem_b, 0)
    edges = use_back(0, sem_edge_own)
    for part in (1, 2):
        gathered(channels(part, 0), 0, None)
    settle_recv(ready_b, tok_b, sem_b, 1)
    edges += use_back(1, sem_edge_rest)
    for part in (1, 2):
        gathered(channels(part, 1), 0, None)
    for source, target, sems in ((prod, recv_p, sem_p), (cotp, recv_g, sem_g), (ready_c, tok_c, sem_c), (ready_b, tok_b, sem_b)):
        for turn in range(2):
            settle_send(source, target, sems, turn)
    for edge in edges:
        edge.wait()
    for turn in range(2):
        for part in (1, 2):
            gathered(channels(part, turn), 1, edge_in[1, :, pl.ds(channels(part, turn), BLOCK)])


def write_kernel(mixed_in, pgrad_in, fgrad_in, mixed, pgrad, fgrad, sems):
    copies = [pltpu.make_async_copy(fgrad_in, fgrad, sems.at[0]), pltpu.make_async_copy(mixed_in, mixed, sems.at[1])]
    for part in range(3):
        span = pl.ds(part * CH, CH)
        copies.append(pltpu.make_async_copy(pgrad_in.at[span], pgrad.at[span], sems.at[2 + part]))
    for copy in copies:
        copy.start()
    for copy in copies:
        copy.wait()


def write_out(*results):
    anywhere = pl.BlockSpec(memory_space=pl.ANY)
    hbm = pl.BlockSpec(memory_space=pltpu.HBM)
    return pl.pallas_call(
        write_kernel,
        out_shape=tuple(pltpu.HBM(result.shape, result.dtype) for result in results),
        in_specs=[anywhere] * 3,
        out_specs=(hbm,) * 3,
        scratch_shapes=[pltpu.SemaphoreType.DMA((5,))],
        compiler_params=pltpu.CompilerParams(vmem_limit_bytes=1 << 20),
        name="write_out",
    )(*results)


def shards(projections, short_filter, long_filter, out_grad):
    vmem = pl.BlockSpec(memory_space=pltpu.VMEM)
    hbm = pl.BlockSpec(memory_space=pltpu.HBM)
    tokens = pltpu.VMEM((CHIPS, 8, A), BF16)
    pair = pltpu.SemaphoreType.DMA((2,))
    sides = pltpu.SemaphoreType.DMA((2, 2))
    swaps = pltpu.SemaphoreType.DMA((CPG, 2))
    operands = (projections, short_filter, long_filter, out_grad, *make_tables())
    mixed, proj_grad, filter_grad = pl.pallas_call(
        mixer_kernel,
        out_shape=(
            jax.ShapeDtypeStruct((CH, A), BF16),
            jax.ShapeDtypeStruct((3 * CH, A), BF16),
            jax.ShapeDtypeStruct((SEQ // 128, 128), F32),
        ),
        in_specs=[hbm] * 9,
        out_specs=(vmem, vmem, vmem),
        scratch_shapes=[
            *[pltpu.VMEM(operand.shape, operand.dtype) for operand in operands],
            pltpu.VMEM((8, 3 * CH), F32),
            pltpu.VMEM((3 * CH, 8), F32),
            pltpu.VMEM((2, A, 128 * (TAPS - 1)), BF16),
            pltpu.VMEM((3 * CH, A), BF16),
            tokens, tokens, tokens, tokens,
            pltpu.VMEM((2, CHIPS * 8, 128), F32),
            pltpu.VMEM((2 * CPG, HALF, A), BF16),
            pltpu.VMEM((4, CPG, CHIPS, A), BF16),
            pltpu.VMEM((2, CPG, CHIPS, A), BF16),
            pltpu.VMEM((2, CPG, CHIPS, A), BF16),
            tokens, tokens, tokens, tokens,
            pltpu.VMEM((ROWS, 2 * A), F32),
            pltpu.VMEM((CPG, ROWS, 2 * A), F32),
            pltpu.VMEM((ROWS, 2 * A), F32),
            pltpu.VMEM((ROWS, 2 * A), BF16),
            pltpu.VMEM((2 * HALF, A), BF16),
            pltpu.VMEM((2 * A, 2 * A), BF16),
            pltpu.VMEM((3 * CH, A), BF16),
            pltpu.VMEM((2, 16, 3 * CH), BF16),
            pltpu.VMEM((2, 16, 3 * CH), BF16),
            pltpu.VMEM((2, 16, CH), BF16),
            pltpu.SemaphoreType.REGULAR((1,)),
            pltpu.SemaphoreType.DMA((14,)),
            pair, pair, sides, sides, pair, sides, sides, sides, sides,
            swaps, swaps, swaps, swaps,
            pltpu.SemaphoreType.DMA((4,)),
        ],
        compiler_params=pltpu.CompilerParams(collective_id=0, has_side_effects=True, vmem_limit_bytes=44 << 20),
        name="mixer",
    )(*[pltpu.with_memory_space_constraint(operand, pltpu.HBM) for operand in operands])
    mixed, proj_grad, filter_grad = write_out(mixed, proj_grad, filter_grad)
    return (mixed, proj_grad, filter_grad.reshape(1, SEQ))


def solution(mesh):
    placed = (P(None, ("dp", "ctx")), P(), P(("dp", "ctx"), None), P(None, ("dp", "ctx")))
    return jax.shard_map(
        shards,
        mesh=mesh,
        in_specs=placed,
        out_specs=(P(None, ("dp", "ctx")), P(None, ("dp", "ctx")), P(("dp", "ctx"), None)),
        check_vma=False,
    )
```

```python
import functools
import math

import jax
import jax.numpy as jnp
import numpy as np
from jax import lax
from jax.experimental import pallas as pl
from jax.experimental.pallas import tpu as pltpu
from jax.sharding import PartitionSpec as P

CPG = 4
TAPS = 7
LANES = 32
CH = 1024
SEQ = 65536
PAD = 2 * SEQ
A = 256
B = 512
HALF = 256
ROWS = 272
CHIPS = 128
DEVICES = 256
SCALE = SEQ ** -0.5
BLOCK = 512
SIDE = 64
NT = (((1,), (1,)), ((), ()))
TN = (((0,), (0,)), ((), ()))
F32 = jnp.float32
BF16 = jnp.bfloat16


def make_tables():
    order = np.concatenate([np.arange(0, HALF, 2), np.arange(1, HALF, 2)])
    d = np.arange(HALF)[:, None]
    outer = 2 * np.pi * ((d * order[None, :]) % B) / B
    cos_outer, sin_outer = np.cos(outer), np.sin(outer)
    sign = 1.0 - 2.0 * (order % 2)
    spread = np.zeros((2 * HALF + 16, HALF))
    spread[:HALF] = cos_outer
    spread[HALF : 2 * HALF] = -sin_outer
    spread[2 * HALF] = sign
    gather = np.zeros((HALF, 2 * HALF))
    gather[:, :HALF] = 2 * cos_outer.T
    gather[:, 0] = 1.0
    gather[:, HALF:] = -2 * sin_outer.T
    gather[:, HALF] = sign
    e = np.arange(A)
    inner = 2 * np.pi * ((e[:, None] * e[None, :]) % A) / A
    cos_inner, sin_inner = np.cos(inner), np.sin(inner)
    mix = np.block([[cos_inner, -sin_inner], [sin_inner, cos_inner]])
    twist = 2 * np.pi * (np.arange(ROWS)[:, None] * e[None, :]) / PAD
    return (
        jnp.asarray(spread.astype(np.float32), BF16),
        jnp.asarray(gather.astype(np.float32), BF16),
        jnp.asarray(mix.astype(np.float32), BF16),
        jnp.asarray(np.cos(twist).astype(np.float32)),
        jnp.asarray(np.sin(twist).astype(np.float32)),
    )


def place(index):
    return (index // LANES, index % LANES)


def signal(sem, index):
    pl.semaphore_signal(sem, inc=1, device_id=place(index), device_id_type=pl.DeviceIdType.MESH)


def remote(source, target, sems, index):
    return pltpu.make_async_remote_copy(
        source, target, sems.at[0], sems.at[1], device_id=place(index), device_id_type=pl.DeviceIdType.MESH
    )


def dot(first, second):
    return jnp.dot(first, second, preferred_element_type=F32)


def one_hot(shape, offset, limit):
    row = lax.broadcasted_iota(jnp.int32, shape, 0)
    lane = lax.broadcasted_iota(jnp.int32, shape, 1)
    return ((lane == row + offset) & (row < limit)).astype(F32).astype(BF16)


def mixer_kernel(
    proj_hbm, taps_hbm, filt_hbm, grad_hbm, spread_hbm, gather_hbm, mix_hbm, cos_hbm, sin_hbm,
    mixed, pgrad, fgrad,
    proj, taps, filt, grad, spread, gather, mix, cos_twist, sin_twist, padded,
    weights, shift, feat, prod, cotp, recv_p, recv_g, fold, signals, swap_out, swap_in, kept, ready_c, ready_b, tok_c, tok_b,
    fspec, kspec, cross, bins, rows, mixback, dfeat, edge_out, edge_in, edge_q,
    rounds, loads, sem_edge, sem_edge_q, sem_edge_own, sem_edge_rest, sem_first, sem_p, sem_g, sem_c, sem_b,
    swap_p, swap_g, swap_c, swap_b, own,
):
    me = lax.axis_index("dp") * LANES + lax.axis_index("ctx")
    chip, core = me // 2, me % 2
    high, low = me // 16, me % 16
    side, within = chip // SIDE, chip % SIDE
    twin = chip * 2 + 1 - core
    after, before = (me + 1) % DEVICES, (me + DEVICES - 1) % DEVICES
    mine = pl.ds(pl.multiple_of(core * CHIPS, CHIPS), CHIPS)

    def channels(part, turn):
        return pl.multiple_of(part * CH + (side * (1 - turn) + (1 - side) * turn) * BLOCK, BLOCK)

    def load(source, target, slot):
        copy = pltpu.make_async_copy(source, target, loads.at[slot])
        copy.start()
        return copy

    taps_load = load(taps_hbm, taps, 0)
    parts = {}
    for slot, (part, turn) in enumerate(((1, 0), (2, 0), (1, 1), (2, 1), (0, 0), (0, 1))):
        span = pl.ds(channels(part, turn), BLOCK)
        parts[part, turn] = load(proj_hbm.at[span], proj.at[span], 1 + slot)
    gate = pltpu.get_barrier_semaphore()
    for step in range(1, 16):
        signal(gate, high * 16 + (low + step) % 16)
    for step in range(1, 16):
        signal(gate, ((high + step) % 16) * 16 + low)
    signal(gate, after)
    signal(gate, before)

    later_loads = [
        load(source, target, 7 + slot)
        for slot, (source, target) in enumerate(
            (
                (grad_hbm, grad), (filt_hbm, filt), (spread_hbm, spread), (cos_hbm, cos_twist),
                (sin_hbm, sin_twist), (mix_hbm, mix), (gather_hbm, gather),
                (mix_hbm.at[:A, :A], mixback.at[:A, :A]), (mix_hbm.at[A:, A:], mixback.at[A:, A:]),
                (mix_hbm.at[A:, :A], mixback.at[:A, A:]), (mix_hbm.at[:A, A:], mixback.at[A:, :A]),
            )
        )
    ]

    row = lax.broadcasted_iota(jnp.int32, (A, 128), 0)
    lane = lax.broadcasted_iota(jnp.int32, (A, 128), 1)
    for lag in range(1, TAPS):
        span = slice((lag - 1) * 128, lag * 128)
        shift[0, :, span] = (row == lane + 128 - lag).astype(F32).astype(BF16)
    last = one_hot((16, A), A - TAPS + 1, TAPS - 1)
    first = one_hot((16, A), 0, TAPS - 1)
    ahead = one_hot((16, 128), 128 - TAPS + 1, TAPS - 1)
    behind = one_hot((16, 128), 0, TAPS - 1)

    taps_load.wait()
    padded[...] = jnp.zeros_like(padded)
    padded[:TAPS, :] = taps[...].astype(F32)
    for block in range(0, 3 * CH, 128):
        weights[block : block + 128, :] = jnp.transpose(padded[:, block : block + 128])

    def take_edge(part, turn):
        parts[part, turn].wait()
        span = pl.ds(channels(part, turn), BLOCK)
        edge_out[0, :, span] = lax.dot_general(last, proj[span, :], NT, preferred_element_type=F32).astype(BF16)

    for part, turn in ((1, 0), (2, 0), (1, 1), (2, 1)):
        take_edge(part, turn)
    pl.semaphore_wait(gate, 32)
    tail = pl.ds(CH, 2 * CH)
    edge_kv = remote(edge_out.at[0, :, tail], edge_in.at[0, :, tail], sem_first, after)
    edge_kv.start()
    for step in range(1, 16):
        signal(rounds.at[0], ((high + step) % 16) * 16 + low)

    def filtered(part, turn, half):
        span = pl.ds(channels(part, turn), BLOCK)
        if half == 0:
            prior = lax.dot_general(edge_in[0, :, span], ahead, TN, preferred_element_type=F32).astype(BF16)
            prior = jnp.where(me > 0, prior, jnp.zeros_like(prior))
            window = jnp.concatenate([prior, proj[span, :128]], axis=1)
        else:
            window = proj[span, :]
        scale = weights[span, :]
        lanes = slice(half * 128, half * 128 + 128)
        moved = dot(window, shift[0])
        total = scale[:, 0:1] * proj[span, lanes].astype(F32)
        for lag in range(1, TAPS):
            total = total + scale[:, lag : lag + 1] * moved[:, (lag - 1) * 128 : lag * 128]
        total = total.astype(BF16)
        feat[span, lanes] = total
        return total.astype(F32)

    def chips(turn):
        return pl.ds(pl.multiple_of(channels(0, turn) // 8, SIDE), SIDE)

    def make_product(turn, half):
        keys = filtered(1, turn, half)
        values = filtered(2, turn, half)
        both = (keys * values).reshape(SIDE, 8, 128)
        prod[chips(turn), :, half * 128 : half * 128 + 128] = both.astype(BF16)

    def make_cotangent(turn, half):
        queries = filtered(0, turn, half)
        lanes = slice(half * 128, half * 128 + 128)
        both = (queries * grad[pl.ds(channels(0, turn), BLOCK), lanes].astype(F32)).reshape(SIDE, 8, 128)
        cotp[chips(turn), :, lanes] = both.astype(BF16)

    def send_side(source, target, sems, turn):
        base = (side * (1 - turn) + (1 - side) * turn) * SIDE

        batch = 7 + turn

        def send(step, carry):
            for place_in_batch in range(batch):
                other = base + (within + step * batch + place_in_batch + 1 - turn) % SIDE
                remote(source.at[other], target.at[chip], sems.at[turn], other * 2 + core).start()
            return carry

        lax.fori_loop(0, (SIDE - 1 + turn) // batch, send, 0)

    def keep_own(source, target, slot):
        keep = pltpu.make_async_copy(source.at[chip], target.at[chip], own.at[slot])
        keep.start()
        return keep

    def settle_send(source, target, sems, turn):
        some = pl.ds(0, SIDE - 1 + turn)
        remote(source.at[some], target.at[some], sems.at[turn], ((chip + 1) % CHIPS) * 2 + core).wait_send()

    def settle_recv(source, target, sems, turn):
        some = pl.ds(0, SIDE - 1 + turn)
        remote(source.at[some], target.at[some], sems.at[turn], ((chip + 1) % CHIPS) * 2 + core).wait_recv()

    make_product(0, 1)
    edge_kv.wait()
    make_product(0, 0)
    pl.semaphore_wait(rounds.at[0], 15)
    send_side(prod, recv_p, sem_p, 0)
    keep_p = keep_own(prod, recv_p, 0)
    make_product(1, 1)
    make_product(1, 0)
    send_side(prod, recv_p, sem_p, 1)
    take_edge(0, 0)
    take_edge(0, 1)
    head = pl.ds(0, CH)
    edge_query = remote(edge_out.at[0, :, head], edge_in.at[0, :, head], sem_edge, after)
    edge_query.start()
    later_loads[0].wait()
    make_cotangent(0, 1)
    edge_query.wait()
    make_cotangent(0, 0)
    send_side(cotp, recv_g, sem_g, 0)
    keep_g = keep_own(cotp, recv_g, 1)
    make_cotangent(1, 1)
    make_cotangent(1, 0)
    send_side(cotp, recv_g, sem_g, 1)

    for copy in later_loads[1:]:
        copy.wait()

    def forward(signal_rows):
        raw = dot(spread[...], signal_rows)
        re, im, odd = raw[:HALF], raw[HALF : 2 * HALF], raw[2 * HALF :]
        ct, st = cos_twist[:HALF, :], sin_twist[:HALF, :]
        bins[:HALF, :A] = (re * ct + im * st).astype(BF16)
        bins[:HALF, A:] = (im * ct - re * st).astype(BF16)
        bins[HALF:, :A] = (odd * cos_twist[HALF:, :]).astype(BF16)
        bins[HALF:, A:] = (-odd * sin_twist[HALF:, :]).astype(BF16)
        return dot(bins[...], mix[...])

    def inverse(re, im):
        bins[:, :A] = re.astype(BF16)
        bins[:, A:] = im.astype(BF16)
        back = dot(bins[...], mixback[...])
        re, im = back[:, :A], back[:, A:]
        ct, st = cos_twist[...], sin_twist[...]
        turn_re = re * ct - im * st
        turn_im = im[:HALF] * ct[:HALF] + re[:HALF] * st[:HALF]
        top = lax.broadcasted_iota(jnp.int32, (16, A), 0) == 0
        rows[:HALF, :] = turn_re[:HALF].astype(BF16)
        rows[HALF:, :] = turn_im.astype(BF16)
        rows[HALF : HALF + 16, :] = jnp.where(top, turn_re[HALF:], turn_im[:16]).astype(BF16)
        return dot(gather[...], rows[...]) * (1.0 / PAD)

    def spread_filter(step, carry):
        piece = filt[:, pl.ds(pl.multiple_of(step * 1024, 1024), 1024)].astype(F32)
        fold[0, pl.ds(pl.multiple_of(step * 8, 8), 8), :] = piece.reshape(8, 128)
        return carry

    lax.fori_loop(0, SEQ // 1024, spread_filter, 0)
    for parity in range(2):
        for half in range(2):
            rows[parity * CHIPS : (parity + 1) * CHIPS, half * 128 : half * 128 + 128] = fold[
                0, pl.ds(2 * parity + half, CHIPS, stride=4), :
            ].astype(BF16)
    fspec[...] = forward(rows[:HALF, :])

    def swap_here(stream, channel, sems):
        return remote(
            swap_out.at[stream, channel], signals.at[stream * CPG + channel, mine, :], sems.at[channel], twin
        )

    def swap_back(stream, channel, sems):
        return remote(swap_out.at[2 + stream, channel], swap_in.at[stream, channel], sems.at[channel], twin)

    def unfold(received, stream, sems):
        for half in range(2):
            lanes = slice(half * 128, half * 128 + 128)
            fold[half] = received[:, :, lanes].astype(F32).reshape(CHIPS * 8, 128)
        for channel in range(CPG):
            for half in range(2):
                lanes = slice(half * 128, half * 128 + 128)
                low_set = fold[half, pl.ds(channel, CHIPS, stride=8), :]
                high_set = fold[half, pl.ds(CPG + channel, CHIPS, stride=8), :]
                signals[stream * CPG + channel, mine, lanes] = jnp.where(core == 0, low_set, high_set).astype(BF16)
                swap_out[stream, channel, :, lanes] = jnp.where(core == 0, high_set, low_set).astype(BF16)
            swap_here(stream, channel, sems).start()

    def refold(stream, ready, sems):
        for channel in range(CPG):
            swap_back(stream, channel, sems).wait()
            for half in range(2):
                lanes = slice(half * 128, half * 128 + 128)
                here = kept[stream, channel, :, lanes].astype(F32)
                there = swap_in[stream, channel, :, lanes].astype(F32)
                fold[half, pl.ds(channel, CHIPS, stride=8), :] = jnp.where(core == 0, here, there)
                fold[half, pl.ds(CPG + channel, CHIPS, stride=8), :] = jnp.where(core == 0, there, here)
        for half in range(2):
            ready[:, :, half * 128 : half * 128 + 128] = fold[half].reshape(CHIPS, 8, 128).astype(BF16)

    def put_away(result, stream, channel, sems):
        even, odd = result[:CHIPS], result[CHIPS:]
        kept[stream, channel] = jnp.where(core == 0, even, odd).astype(BF16)
        swap_out[2 + stream, channel] = jnp.where(core == 0, odd, even).astype(BF16)
        swap_back(stream, channel, sems).start()

    keep_p.wait()
    for turn in range(2):
        settle_recv(prod, recv_p, sem_p, turn)
    unfold(recv_p, 0, swap_p)

    def convolve(channel, carry):
        swap_here(0, channel, swap_p).wait()
        spec = forward(signals[channel])
        kspec[channel] = spec
        re, im = spec[:, :A], spec[:, A:]
        f_re, f_im = fspec[:, :A], fspec[:, A:]
        result = inverse((f_re * re - f_im * im) * SCALE, (f_re * im + f_im * re) * SCALE)
        put_away(result, 0, channel, swap_c)
        return carry

    lax.fori_loop(0, CPG, convolve, 0)
    refold(0, ready_c, swap_c)
    for turn in range(2):
        send_side(ready_c, tok_c, sem_c, turn)
    keep_c = keep_own(ready_c, tok_c, 2)

    keep_g.wait()
    for turn in range(2):
        settle_recv(cotp, recv_g, sem_g, turn)
    unfold(recv_g, 1, swap_g)
    cross[...] = jnp.zeros_like(cross)
    for lag in range(1, TAPS):
        span = slice((lag - 1) * 128, lag * 128)
        shift[1, :, span] = (row == lane + lag).astype(F32).astype(BF16)

    def correlate(channel, carry):
        swap_here(1, channel, swap_g).wait()
        spec = forward(signals[CPG + channel])
        re, im = spec[:, :A], spec[:, A:]
        k_re, k_im = kspec[channel, :, :A], kspec[channel, :, A:]
        cross[:, :A] = cross[:, :A] + (k_re * re + k_im * im)
        cross[:, A:] = cross[:, A:] + (k_re * im - k_im * re)
        f_re, f_im = fspec[:, :A], fspec[:, A:]
        result = inverse((f_re * re + f_im * im) * SCALE, (f_re * im - f_im * re) * SCALE)
        put_away(result, 1, channel, swap_b)
        return carry

    lax.fori_loop(0, CPG, correlate, 0)
    refold(1, ready_b, swap_b)
    for turn in range(2):
        send_side(ready_b, tok_b, sem_b, turn)
    keep_b = keep_own(ready_b, tok_b, 3)

    result = inverse(cross[:, :A], cross[:, A:]) * SCALE
    for parity in range(2):
        for half in range(2):
            fgrad[pl.ds(2 * parity + half, CHIPS, stride=4), :] = result[
                parity * CHIPS : (parity + 1) * CHIPS, half * 128 : half * 128 + 128
            ]

    keep_c.wait()
    for turn in range(2):
        settle_recv(ready_c, tok_c, sem_c, turn)

    def use_conv(step, carry):
        span = pl.ds(pl.multiple_of(step * BLOCK, BLOCK), BLOCK)
        conv = tok_c[pl.ds(step * SIDE, SIDE)].astype(F32).reshape(BLOCK, A)
        mixed[span, :] = (feat[span, :].astype(F32) * conv).astype(BF16)
        back = (grad[span, :].astype(F32) * conv).astype(BF16)
        dfeat[span, :] = back
        edge_q[0, :, span] = lax.dot_general(first, back, NT, preferred_element_type=F32).astype(BF16)
        return carry

    lax.fori_loop(0, CH // BLOCK, use_conv, 0)
    edge_back = remote(edge_q.at[0], edge_q.at[1], sem_edge_q, before)
    edge_back.start()

    def gathered(start, half, halo):
        span = pl.ds(pl.multiple_of(start, BLOCK), BLOCK)
        lanes = slice(half * 128, half * 128 + 128)
        if half == 0:
            window = dfeat[span, :]
        else:
            later = lax.dot_general(halo, behind, TN, preferred_element_type=F32).astype(BF16)
            later = jnp.where(me < DEVICES - 1, later, jnp.zeros_like(later))
            window = jnp.concatenate([dfeat[span, 128:], later], axis=1)
        scale = weights[span, :]
        moved = dot(window, shift[1])
        total = scale[:, 0:1] * dfeat[span, lanes].astype(F32)
        for lag in range(1, TAPS):
            total = total + scale[:, lag : lag + 1] * moved[:, (lag - 1) * 128 : lag * 128]
        pgrad[span, lanes] = total.astype(BF16)

    for step in range(CH // BLOCK):
        gathered(step * BLOCK, 0, None)
    edge_back.wait()
    for step in range(CH // BLOCK):
        gathered(step * BLOCK, 1, edge_q[1, :, step * BLOCK : (step + 1) * BLOCK])

    def use_back(turn, sems):
        back = tok_b[chips(turn)].astype(F32).reshape(BLOCK, A)
        for part, other in ((1, 2), (2, 1)):
            result = (feat[pl.ds(channels(other, turn), BLOCK), :].astype(F32) * back).astype(BF16)
            target = pl.ds(channels(part, turn), BLOCK)
            dfeat[target, :] = result
            edge_out[1, :, target] = lax.dot_general(first, result, NT, preferred_element_type=F32).astype(BF16)
        edges = []
        for part in (1, 2):
            target = pl.ds(channels(part, turn), BLOCK)
            edge = remote(edge_out.at[1, :, target], edge_in.at[1, :, target], sems.at[part - 1], before)
            edge.start()
            edges.append(edge)
        return edges

    keep_b.wait()
    settle_recv(ready_b, tok_b, sem_b, 0)
    edges = use_back(0, sem_edge_own)
    for part in (1, 2):
        gathered(channels(part, 0), 0, None)

    ahead_side = after // 2 // SIDE
    first_start = ahead_side * BLOCK
    second_start = (1 - ahead_side) * BLOCK

    def finish(start):
        for part in (1, 2):
            begin = pl.multiple_of(part * CH + start, BLOCK)
            gathered(begin, 1, edge_in[1, :, pl.ds(begin, BLOCK)])

    for edge in edges:
        edge.wait()
    finish(first_start)
    settle_recv(ready_b, tok_b, sem_b, 1)
    edges_rest = use_back(1, sem_edge_rest)
    for part in (1, 2):
        gathered(channels(part, 1), 0, None)
    for source, target, sems in ((prod, recv_p, sem_p), (cotp, recv_g, sem_g), (ready_c, tok_c, sem_c), (ready_b, tok_b, sem_b)):
        for turn in range(2):
            settle_send(source, target, sems, turn)
    for edge in edges_rest:
        edge.wait()
    finish(second_start)

    @pl.when(ahead_side != side)
    def _():
        finish(first_start)


def write_kernel(mixed_in, pgrad_in, fgrad_in, mixed, pgrad, fgrad, sems):
    copies = [pltpu.make_async_copy(fgrad_in, fgrad, sems.at[0]), pltpu.make_async_copy(mixed_in, mixed, sems.at[1])]
    for part in range(3):
        span = pl.ds(part * CH, CH)
        copies.append(pltpu.make_async_copy(pgrad_in.at[span], pgrad.at[span], sems.at[2 + part]))
    for copy in copies:
        copy.start()
    for copy in copies:
        copy.wait()


def write_out(*results):
    anywhere = pl.BlockSpec(memory_space=pl.ANY)
    hbm = pl.BlockSpec(memory_space=pltpu.HBM)
    return pl.pallas_call(
        write_kernel,
        out_shape=tuple(pltpu.HBM(result.shape, result.dtype) for result in results),
        in_specs=[anywhere] * 3,
        out_specs=(hbm,) * 3,
        scratch_shapes=[pltpu.SemaphoreType.DMA((5,))],
        compiler_params=pltpu.CompilerParams(vmem_limit_bytes=1 << 20),
        name="write_out",
    )(*results)


def shards(projections, short_filter, long_filter, out_grad):
    vmem = pl.BlockSpec(memory_space=pltpu.VMEM)
    hbm = pl.BlockSpec(memory_space=pltpu.HBM)
    tokens = pltpu.VMEM((CHIPS, 8, A), BF16)
    pair = pltpu.SemaphoreType.DMA((2,))
    sides = pltpu.SemaphoreType.DMA((2, 2))
    swaps = pltpu.SemaphoreType.DMA((CPG, 2))
    operands = (projections, short_filter, long_filter, out_grad, *make_tables())
    mixed, proj_grad, filter_grad = pl.pallas_call(
        mixer_kernel,
        out_shape=(
            jax.ShapeDtypeStruct((CH, A), BF16),
            jax.ShapeDtypeStruct((3 * CH, A), BF16),
            jax.ShapeDtypeStruct((SEQ // 128, 128), F32),
        ),
        in_specs=[hbm] * 9,
        out_specs=(vmem, vmem, vmem),
        scratch_shapes=[
            *[pltpu.VMEM(operand.shape, operand.dtype) for operand in operands],
            pltpu.VMEM((8, 3 * CH), F32),
            pltpu.VMEM((3 * CH, 8), F32),
            pltpu.VMEM((2, A, 128 * (TAPS - 1)), BF16),
            pltpu.VMEM((3 * CH, A), BF16),
            tokens, tokens, tokens, tokens,
            pltpu.VMEM((2, CHIPS * 8, 128), F32),
            pltpu.VMEM((2 * CPG, HALF, A), BF16),
            pltpu.VMEM((4, CPG, CHIPS, A), BF16),
            pltpu.VMEM((2, CPG, CHIPS, A), BF16),
            pltpu.VMEM((2, CPG, CHIPS, A), BF16),
            tokens, tokens, tokens, tokens,
            pltpu.VMEM((ROWS, 2 * A), F32),
            pltpu.VMEM((CPG, ROWS, 2 * A), F32),
            pltpu.VMEM((ROWS, 2 * A), F32),
            pltpu.VMEM((ROWS, 2 * A), BF16),
            pltpu.VMEM((2 * HALF, A), BF16),
            pltpu.VMEM((2 * A, 2 * A), BF16),
            pltpu.VMEM((3 * CH, A), BF16),
            pltpu.VMEM((2, 16, 3 * CH), BF16),
            pltpu.VMEM((2, 16, 3 * CH), BF16),
            pltpu.VMEM((2, 16, CH), BF16),
            pltpu.SemaphoreType.REGULAR((1,)),
            pltpu.SemaphoreType.DMA((18,)),
            pair, pair, sides, sides, pair, sides, sides, sides, sides,
            swaps, swaps, swaps, swaps,
            pltpu.SemaphoreType.DMA((4,)),
        ],
        compiler_params=pltpu.CompilerParams(collective_id=0, has_side_effects=True, vmem_limit_bytes=44 << 20),
        name="mixer",
    )(*[pltpu.with_memory_space_constraint(operand, pltpu.HBM) for operand in operands])
    mixed, proj_grad, filter_grad = write_out(mixed, proj_grad, filter_grad)
    return (mixed, proj_grad, filter_grad.reshape(1, SEQ))


def solution(mesh):
    placed = (P(None, ("dp", "ctx")), P(), P(("dp", "ctx"), None), P(None, ("dp", "ctx")))
    return jax.shard_map(
        shards,
        mesh=mesh,
        in_specs=placed,
        out_specs=(P(None, ("dp", "ctx")), P(None, ("dp", "ctx")), P(("dp", "ctx"), None)),
        check_vma=False,
    )
```

```python
import functools
import math

import jax
import jax.numpy as jnp
import numpy as np
from jax import lax
from jax.experimental import pallas as pl
from jax.experimental.pallas import tpu as pltpu
from jax.sharding import PartitionSpec as P

CPG = 4
TAPS = 7
LANES = 32
CH = 1024
SEQ = 65536
PAD = 2 * SEQ
A = 256
B = 512
HALF = 256
ROWS = 272
CHIPS = 128
DEVICES = 256
SCALE = SEQ ** -0.5
BLOCK = 512
SIDE = 64
NT = (((1,), (1,)), ((), ()))
TN = (((0,), (0,)), ((), ()))
F32 = jnp.float32
BF16 = jnp.bfloat16


def make_tables():
    order = np.concatenate([np.arange(0, HALF, 2), np.arange(1, HALF, 2)])
    d = np.arange(HALF)[:, None]
    outer = 2 * np.pi * ((d * order[None, :]) % B) / B
    cos_outer, sin_outer = np.cos(outer), np.sin(outer)
    sign = 1.0 - 2.0 * (order % 2)
    spread = np.zeros((2 * HALF + 16, HALF))
    spread[:HALF] = cos_outer
    spread[HALF : 2 * HALF] = -sin_outer
    spread[2 * HALF] = sign
    gather = np.zeros((HALF, 2 * HALF))
    gather[:, :HALF] = 2 * cos_outer.T
    gather[:, 0] = 1.0
    gather[:, HALF:] = -2 * sin_outer.T
    gather[:, HALF] = sign
    e = np.arange(A)
    inner = 2 * np.pi * ((e[:, None] * e[None, :]) % A) / A
    cos_inner, sin_inner = np.cos(inner), np.sin(inner)
    mix = np.block([[cos_inner, -sin_inner], [sin_inner, cos_inner]])
    twist = 2 * np.pi * (np.arange(ROWS)[:, None] * e[None, :]) / PAD
    return (
        jnp.asarray(spread.astype(np.float32), BF16),
        jnp.asarray(gather.astype(np.float32), BF16),
        jnp.asarray(mix.astype(np.float32), BF16),
        jnp.asarray(np.cos(twist).astype(np.float32)),
        jnp.asarray(np.sin(twist).astype(np.float32)),
    )


def place(index):
    return (index // LANES, index % LANES)


def signal(sem, index):
    pl.semaphore_signal(sem, inc=1, device_id=place(index), device_id_type=pl.DeviceIdType.MESH)


def remote(source, target, sems, index):
    return pltpu.make_async_remote_copy(
        source, target, sems.at[0], sems.at[1], device_id=place(index), device_id_type=pl.DeviceIdType.MESH
    )


def dot(first, second):
    return jnp.dot(first, second, preferred_element_type=F32)


def one_hot(shape, offset, limit):
    row = lax.broadcasted_iota(jnp.int32, shape, 0)
    lane = lax.broadcasted_iota(jnp.int32, shape, 1)
    return ((lane == row + offset) & (row < limit)).astype(F32).astype(BF16)


def mixer_kernel(
    proj_hbm, taps_hbm, filt_hbm, grad_hbm, spread_hbm, gather_hbm, mix_hbm, cos_hbm, sin_hbm,
    mixed, pgrad, fgrad,
    proj, taps, filt, grad, spread, gather, mix, cos_twist, sin_twist, padded,
    weights, shift, feat, prod, cotp, recv_p, recv_g, fold, signals, swap_out, swap_in, kept, ready_c, ready_b, tok_c, tok_b,
    fspec, kspec, cross, bins, rows, mixback, dfeat, edge_out, edge_in, edge_q,
    rounds, loads, sem_edge, sem_edge_q, sem_edge_own, sem_edge_rest, sem_first, sem_p, sem_g, sem_c, sem_b,
    swap_p, swap_g, swap_c, swap_b, own,
):
    me = lax.axis_index("dp") * LANES + lax.axis_index("ctx")
    chip, core = me // 2, me % 2
    high, low = me // 16, me % 16
    side, within = chip // SIDE, chip % SIDE
    twin = chip * 2 + 1 - core
    after, before = (me + 1) % DEVICES, (me + DEVICES - 1) % DEVICES
    mine = pl.ds(pl.multiple_of(core * CHIPS, CHIPS), CHIPS)

    def channels(part, turn):
        return pl.multiple_of(part * CH + (side * (1 - turn) + (1 - side) * turn) * BLOCK, BLOCK)

    def load(source, target, slot):
        copy = pltpu.make_async_copy(source, target, loads.at[slot])
        copy.start()
        return copy

    taps_load = load(taps_hbm, taps, 0)
    parts = {}
    for slot, (part, turn) in enumerate(((1, 0), (2, 0), (1, 1), (2, 1), (0, 0), (0, 1))):
        span = pl.ds(channels(part, turn), BLOCK)
        parts[part, turn] = load(proj_hbm.at[span], proj.at[span], 1 + slot)
    gate = pltpu.get_barrier_semaphore()
    for step in range(1, 16):
        signal(gate, high * 16 + (low + step) % 16)
    for step in range(1, 16):
        signal(gate, ((high + step) % 16) * 16 + low)
    signal(gate, after)
    signal(gate, before)

    later_loads = [
        load(source, target, 7 + slot)
        for slot, (source, target) in enumerate(
            (
                (grad_hbm, grad), (filt_hbm, filt), (spread_hbm, spread), (cos_hbm, cos_twist),
                (sin_hbm, sin_twist), (mix_hbm, mix), (gather_hbm, gather),
                (mix_hbm.at[:A, :A], mixback.at[:A, :A]), (mix_hbm.at[A:, A:], mixback.at[A:, A:]),
                (mix_hbm.at[A:, :A], mixback.at[:A, A:]), (mix_hbm.at[:A, A:], mixback.at[A:, :A]),
            )
        )
    ]

    row = lax.broadcasted_iota(jnp.int32, (A, 128), 0)
    lane = lax.broadcasted_iota(jnp.int32, (A, 128), 1)
    for lag in range(1, TAPS):
        span = slice((lag - 1) * 128, lag * 128)
        shift[0, :, span] = (row == lane + 128 - lag).astype(F32).astype(BF16)
    last = one_hot((16, A), A - TAPS + 1, TAPS - 1)
    first = one_hot((16, A), 0, TAPS - 1)
    ahead = one_hot((16, 128), 128 - TAPS + 1, TAPS - 1)
    behind = one_hot((16, 128), 0, TAPS - 1)

    taps_load.wait()
    padded[...] = jnp.zeros_like(padded)
    padded[:TAPS, :] = taps[...].astype(F32)
    for block in range(0, 3 * CH, 128):
        weights[block : block + 128, :] = jnp.transpose(padded[:, block : block + 128])

    def take_edge(part, turn):
        parts[part, turn].wait()
        span = pl.ds(channels(part, turn), BLOCK)
        edge_out[0, :, span] = lax.dot_general(last, proj[span, :], NT, preferred_element_type=F32).astype(BF16)

    for part, turn in ((1, 0), (2, 0), (1, 1), (2, 1)):
        take_edge(part, turn)
    pl.semaphore_wait(gate, 32)
    tail = pl.ds(CH, 2 * CH)
    edge_kv = remote(edge_out.at[0, :, tail], edge_in.at[0, :, tail], sem_first, after)
    edge_kv.start()
    for step in range(1, 16):
        signal(rounds.at[0], ((high + step) % 16) * 16 + low)

    def filtered(part, turn, half, quarter=None):
        span = pl.ds(channels(part, turn), BLOCK)
        if quarter is not None:
            span = pl.ds(pl.multiple_of(channels(part, turn) + quarter * (BLOCK // 2), BLOCK // 2), BLOCK // 2)
        if half == 0:
            prior = lax.dot_general(edge_in[0, :, span], ahead, TN, preferred_element_type=F32).astype(BF16)
            prior = jnp.where(me > 0, prior, jnp.zeros_like(prior))
            window = jnp.concatenate([prior, proj[span, :128]], axis=1)
        else:
            window = proj[span, :]
        scale = weights[span, :]
        lanes = slice(half * 128, half * 128 + 128)
        moved = dot(window, shift[0])
        total = scale[:, 0:1] * proj[span, lanes].astype(F32)
        for lag in range(1, TAPS):
            total = total + scale[:, lag : lag + 1] * moved[:, (lag - 1) * 128 : lag * 128]
        total = total.astype(BF16)
        feat[span, lanes] = total
        return total.astype(F32)

    def chips(turn):
        return pl.ds(pl.multiple_of(channels(0, turn) // 8, SIDE), SIDE)

    def make_product(turn, half, quarter=None):
        keys = filtered(1, turn, half, quarter)
        values = filtered(2, turn, half, quarter)
        where = chips(turn)
        if quarter is not None:
            where = pl.ds(pl.multiple_of(channels(0, turn) // 8 + quarter * (SIDE // 2), SIDE // 2), SIDE // 2)
        both = (keys * values).reshape(-1, 8, 128)
        prod[where, :, half * 128 : half * 128 + 128] = both.astype(BF16)

    def make_cotangent(turn, half):
        queries = filtered(0, turn, half)
        lanes = slice(half * 128, half * 128 + 128)
        both = (queries * grad[pl.ds(channels(0, turn), BLOCK), lanes].astype(F32)).reshape(SIDE, 8, 128)
        cotp[chips(turn), :, lanes] = both.astype(BF16)

    def send_side(source, target, sems, turn):
        base = (side * (1 - turn) + (1 - side) * turn) * SIDE

        batch = 7 + turn

        def send(step, carry):
            for place_in_batch in range(batch):
                other = base + (within + step * batch + place_in_batch + 1 - turn) % SIDE
                remote(source.at[other], target.at[chip], sems.at[turn], other * 2 + core).start()
            return carry

        lax.fori_loop(0, (SIDE - 1 + turn) // batch, send, 0)

    def send_quarter(source, target, sems, quarter, skip):
        base = side * SIDE + quarter * (SIDE // 2)

        def send(step, carry):
            other = base + (within + step) % (SIDE // 2)
            remote(source.at[other], target.at[chip], sems.at[0], other * 2 + core).start()
            return carry

        lax.fori_loop(skip, SIDE // 2, send, 0)

    def keep_own(source, target, slot):
        keep = pltpu.make_async_copy(source.at[chip], target.at[chip], own.at[slot])
        keep.start()
        return keep

    def settle_send(source, target, sems, turn):
        some = pl.ds(0, SIDE - 1 + turn)
        remote(source.at[some], target.at[some], sems.at[turn], ((chip + 1) % CHIPS) * 2 + core).wait_send()

    def settle_recv(source, target, sems, turn):
        some = pl.ds(0, SIDE - 1 + turn)
        remote(source.at[some], target.at[some], sems.at[turn], ((chip + 1) % CHIPS) * 2 + core).wait_recv()

    near = within // (SIDE // 2)
    make_product(0, 1, near)
    edge_kv.wait()
    make_product(0, 0, near)
    pl.semaphore_wait(rounds.at[0], 15)
    send_quarter(prod, recv_p, sem_p, near, 1)
    keep_p = keep_own(prod, recv_p, 0)
    make_product(0, 1, 1 - near)
    make_product(0, 0, 1 - near)
    send_quarter(prod, recv_p, sem_p, 1 - near, 0)
    make_product(1, 1)
    make_product(1, 0)
    send_side(prod, recv_p, sem_p, 1)
    take_edge(0, 0)
    take_edge(0, 1)
    head = pl.ds(0, CH)
    edge_query = remote(edge_out.at[0, :, head], edge_in.at[0, :, head], sem_edge, after)
    edge_query.start()
    later_loads[0].wait()
    make_cotangent(0, 1)
    edge_query.wait()
    make_cotangent(0, 0)
    send_side(cotp, recv_g, sem_g, 0)
    keep_g = keep_own(cotp, recv_g, 1)
    make_cotangent(1, 1)
    make_cotangent(1, 0)
    send_side(cotp, recv_g, sem_g, 1)

    for copy in later_loads[1:]:
        copy.wait()

    def forward(signals_rows):
        raws = [dot(spread[...], signal_rows) for signal_rows in signals_rows]
        ct, st = cos_twist[:HALF, :], sin_twist[:HALF, :]
        for slot, raw in enumerate(raws):
            re, im, odd = raw[:HALF], raw[HALF : 2 * HALF], raw[2 * HALF :]
            bins[slot, :HALF, :A] = (re * ct + im * st).astype(BF16)
            bins[slot, :HALF, A:] = (im * ct - re * st).astype(BF16)
            bins[slot, HALF:, :A] = (odd * cos_twist[HALF:, :]).astype(BF16)
            bins[slot, HALF:, A:] = (-odd * sin_twist[HALF:, :]).astype(BF16)
        return [dot(bins[slot], mix[...]) for slot in range(len(raws))]

    def inverse(spectra):
        for slot, (re, im) in enumerate(spectra):
            bins[slot, :, :A] = re.astype(BF16)
            bins[slot, :, A:] = im.astype(BF16)
        backs = [dot(bins[slot], mixback[...]) for slot in range(len(spectra))]
        ct, st = cos_twist[...], sin_twist[...]
        top = lax.broadcasted_iota(jnp.int32, (16, A), 0) == 0
        for slot, back in enumerate(backs):
            re, im = back[:, :A], back[:, A:]
            turn_re = re * ct - im * st
            turn_im = im[:HALF] * ct[:HALF] + re[:HALF] * st[:HALF]
            rows[slot, :HALF, :] = turn_re[:HALF].astype(BF16)
            rows[slot, HALF:, :] = turn_im.astype(BF16)
            rows[slot, HALF : HALF + 16, :] = jnp.where(top, turn_re[HALF:], turn_im[:16]).astype(BF16)
        return [dot(gather[...], rows[slot]) * (1.0 / PAD) for slot in range(len(spectra))]

    def spread_filter(step, carry):
        piece = filt[:, pl.ds(pl.multiple_of(step * 1024, 1024), 1024)].astype(F32)
        fold[0, pl.ds(pl.multiple_of(step * 8, 8), 8), :] = piece.reshape(8, 128)
        return carry

    lax.fori_loop(0, SEQ // 1024, spread_filter, 0)
    for parity in range(2):
        for half in range(2):
            rows[0, parity * CHIPS : (parity + 1) * CHIPS, half * 128 : half * 128 + 128] = fold[
                0, pl.ds(2 * parity + half, CHIPS, stride=4), :
            ].astype(BF16)
    fspec[...] = forward([rows[0, :HALF, :]])[0]

    def swap_here(stream, channel, sems):
        return remote(
            swap_out.at[stream, channel], signals.at[stream * CPG + channel, mine, :], sems.at[channel], twin
        )

    def swap_back(stream, channel, sems):
        return remote(swap_out.at[2 + stream, channel], swap_in.at[stream, channel], sems.at[channel], twin)

    def unfold(received, stream, sems):
        for half in range(2):
            lanes = slice(half * 128, half * 128 + 128)
            fold[half] = received[:, :, lanes].astype(F32).reshape(CHIPS * 8, 128)
        for channel in range(CPG):
            for half in range(2):
                lanes = slice(half * 128, half * 128 + 128)
                low_set = fold[half, pl.ds(channel, CHIPS, stride=8), :]
                high_set = fold[half, pl.ds(CPG + channel, CHIPS, stride=8), :]
                signals[stream * CPG + channel, mine, lanes] = jnp.where(core == 0, low_set, high_set).astype(BF16)
                swap_out[stream, channel, :, lanes] = jnp.where(core == 0, high_set, low_set).astype(BF16)
            swap_here(stream, channel, sems).start()

    def refold(stream, ready, sems):
        for channel in range(CPG):
            swap_back(stream, channel, sems).wait()
            for half in range(2):
                lanes = slice(half * 128, half * 128 + 128)
                here = kept[stream, channel, :, lanes].astype(F32)
                there = swap_in[stream, channel, :, lanes].astype(F32)
                fold[half, pl.ds(channel, CHIPS, stride=8), :] = jnp.where(core == 0, here, there)
                fold[half, pl.ds(CPG + channel, CHIPS, stride=8), :] = jnp.where(core == 0, there, here)
        for half in range(2):
            ready[:, :, half * 128 : half * 128 + 128] = fold[half].reshape(CHIPS, 8, 128).astype(BF16)

    def put_away(result, stream, channel, sems):
        even, odd = result[:CHIPS], result[CHIPS:]
        kept[stream, channel] = jnp.where(core == 0, even, odd).astype(BF16)
        swap_out[2 + stream, channel] = jnp.where(core == 0, odd, even).astype(BF16)
        swap_back(stream, channel, sems).start()

    keep_p.wait()
    for turn in range(2):
        settle_recv(prod, recv_p, sem_p, turn)
    unfold(recv_p, 0, swap_p)

    def convolve(step, carry):
        pair = [step * 2, step * 2 + 1]
        for channel in pair:
            swap_here(0, channel, swap_p).wait()
        spectra = []
        for channel, spec in zip(pair, forward([signals[channel] for channel in pair])):
            kspec[channel] = spec
            re, im = spec[:, :A], spec[:, A:]
            f_re, f_im = fspec[:, :A], fspec[:, A:]
            spectra.append(((f_re * re - f_im * im) * SCALE, (f_re * im + f_im * re) * SCALE))
        for channel, result in zip(pair, inverse(spectra)):
            put_away(result, 0, channel, swap_c)
        return carry

    lax.fori_loop(0, CPG // 2, convolve, 0)
    refold(0, ready_c, swap_c)
    for turn in range(2):
        send_side(ready_c, tok_c, sem_c, turn)
    keep_c = keep_own(ready_c, tok_c, 2)

    keep_g.wait()
    for turn in range(2):
        settle_recv(cotp, recv_g, sem_g, turn)
    unfold(recv_g, 1, swap_g)
    cross[...] = jnp.zeros_like(cross)
    for lag in range(1, TAPS):
        span = slice((lag - 1) * 128, lag * 128)
        shift[1, :, span] = (row == lane + lag).astype(F32).astype(BF16)

    def correlate(step, carry):
        pair = [step * 2, step * 2 + 1]
        for channel in pair:
            swap_here(1, channel, swap_g).wait()
        spectra = []
        for channel, spec in zip(pair, forward([signals[CPG + channel] for channel in pair])):
            re, im = spec[:, :A], spec[:, A:]
            k_re, k_im = kspec[channel, :, :A], kspec[channel, :, A:]
            cross[:, :A] = cross[:, :A] + (k_re * re + k_im * im)
            cross[:, A:] = cross[:, A:] + (k_re * im - k_im * re)
            f_re, f_im = fspec[:, :A], fspec[:, A:]
            spectra.append(((f_re * re + f_im * im) * SCALE, (f_re * im - f_im * re) * SCALE))
        for channel, result in zip(pair, inverse(spectra)):
            put_away(result, 1, channel, swap_b)
        return carry

    lax.fori_loop(0, CPG // 2, correlate, 0)
    refold(1, ready_b, swap_b)
    for turn in range(2):
        send_side(ready_b, tok_b, sem_b, turn)
    keep_b = keep_own(ready_b, tok_b, 3)

    result = inverse([(cross[:, :A], cross[:, A:])])[0] * SCALE
    for parity in range(2):
        for half in range(2):
            fgrad[pl.ds(2 * parity + half, CHIPS, stride=4), :] = result[
                parity * CHIPS : (parity + 1) * CHIPS, half * 128 : half * 128 + 128
            ]

    keep_c.wait()
    for turn in range(2):
        settle_recv(ready_c, tok_c, sem_c, turn)

    def use_conv(step, carry):
        span = pl.ds(pl.multiple_of(step * BLOCK, BLOCK), BLOCK)
        conv = tok_c[pl.ds(step * SIDE, SIDE)].astype(F32).reshape(BLOCK, A)
        mixed[span, :] = (feat[span, :].astype(F32) * conv).astype(BF16)
        back = (grad[span, :].astype(F32) * conv).astype(BF16)
        dfeat[span, :] = back
        edge_q[0, :, span] = lax.dot_general(first, back, NT, preferred_element_type=F32).astype(BF16)
        return carry

    lax.fori_loop(0, CH // BLOCK, use_conv, 0)
    edge_back = remote(edge_q.at[0], edge_q.at[1], sem_edge_q, before)
    edge_back.start()

    def gathered(start, half, halo):
        span = pl.ds(pl.multiple_of(start, BLOCK), BLOCK)
        lanes = slice(half * 128, half * 128 + 128)
        if half == 0:
            window = dfeat[span, :]
        else:
            later = lax.dot_general(halo, behind, TN, preferred_element_type=F32).astype(BF16)
            later = jnp.where(me < DEVICES - 1, later, jnp.zeros_like(later))
            window = jnp.concatenate([dfeat[span, 128:], later], axis=1)
        scale = weights[span, :]
        moved = dot(window, shift[1])
        total = scale[:, 0:1] * dfeat[span, lanes].astype(F32)
        for lag in range(1, TAPS):
            total = total + scale[:, lag : lag + 1] * moved[:, (lag - 1) * 128 : lag * 128]
        pgrad[span, lanes] = total.astype(BF16)

    for step in range(CH // BLOCK):
        gathered(step * BLOCK, 0, None)
    edge_back.wait()
    for step in range(CH // BLOCK):
        gathered(step * BLOCK, 1, edge_q[1, :, step * BLOCK : (step + 1) * BLOCK])

    def use_back(turn, sems):
        back = tok_b[chips(turn)].astype(F32).reshape(BLOCK, A)
        for part, other in ((1, 2), (2, 1)):
            result = (feat[pl.ds(channels(other, turn), BLOCK), :].astype(F32) * back).astype(BF16)
            target = pl.ds(channels(part, turn), BLOCK)
            dfeat[target, :] = result
            edge_out[1, :, target] = lax.dot_general(first, result, NT, preferred_element_type=F32).astype(BF16)
        edges = []
        for part in (1, 2):
            target = pl.ds(channels(part, turn), BLOCK)
            edge = remote(edge_out.at[1, :, target], edge_in.at[1, :, target], sems.at[part - 1], before)
            edge.start()
            edges.append(edge)
        return edges

    keep_b.wait()
    settle_recv(ready_b, tok_b, sem_b, 0)
    edges = use_back(0, sem_edge_own)
    for part in (1, 2):
        gathered(channels(part, 0), 0, None)

    ahead_side = after // 2 // SIDE
    first_start = ahead_side * BLOCK
    second_start = (1 - ahead_side) * BLOCK

    def finish(start):
        for part in (1, 2):
            begin = pl.multiple_of(part * CH + start, BLOCK)
            gathered(begin, 1, edge_in[1, :, pl.ds(begin, BLOCK)])

    for edge in edges:
        edge.wait()
    finish(first_start)
    settle_recv(ready_b, tok_b, sem_b, 1)
    edges_rest = use_back(1, sem_edge_rest)
    for part in (1, 2):
        gathered(channels(part, 1), 0, None)
    for source, target, sems in ((prod, recv_p, sem_p), (cotp, recv_g, sem_g), (ready_c, tok_c, sem_c), (ready_b, tok_b, sem_b)):
        for turn in range(2):
            settle_send(source, target, sems, turn)
    for edge in edges_rest:
        edge.wait()
    finish(second_start)

    @pl.when(ahead_side != side)
    def _():
        finish(first_start)


def write_kernel(mixed_in, pgrad_in, fgrad_in, mixed, pgrad, fgrad, sems):
    copies = [pltpu.make_async_copy(fgrad_in, fgrad, sems.at[0]), pltpu.make_async_copy(mixed_in, mixed, sems.at[1])]
    for part in range(3):
        span = pl.ds(part * CH, CH)
        copies.append(pltpu.make_async_copy(pgrad_in.at[span], pgrad.at[span], sems.at[2 + part]))
    for copy in copies:
        copy.start()
    for copy in copies:
        copy.wait()


def write_out(*results):
    anywhere = pl.BlockSpec(memory_space=pl.ANY)
    hbm = pl.BlockSpec(memory_space=pltpu.HBM)
    return pl.pallas_call(
        write_kernel,
        out_shape=tuple(pltpu.HBM(result.shape, result.dtype) for result in results),
        in_specs=[anywhere] * 3,
        out_specs=(hbm,) * 3,
        scratch_shapes=[pltpu.SemaphoreType.DMA((5,))],
        compiler_params=pltpu.CompilerParams(vmem_limit_bytes=1 << 20),
        name="write_out",
    )(*results)


def shards(projections, short_filter, long_filter, out_grad):
    vmem = pl.BlockSpec(memory_space=pltpu.VMEM)
    hbm = pl.BlockSpec(memory_space=pltpu.HBM)
    tokens = pltpu.VMEM((CHIPS, 8, A), BF16)
    pair = pltpu.SemaphoreType.DMA((2,))
    sides = pltpu.SemaphoreType.DMA((2, 2))
    swaps = pltpu.SemaphoreType.DMA((CPG, 2))
    operands = (projections, short_filter, long_filter, out_grad, *make_tables())
    mixed, proj_grad, filter_grad = pl.pallas_call(
        mixer_kernel,
        out_shape=(
            jax.ShapeDtypeStruct((CH, A), BF16),
            jax.ShapeDtypeStruct((3 * CH, A), BF16),
            jax.ShapeDtypeStruct((SEQ // 128, 128), F32),
        ),
        in_specs=[hbm] * 9,
        out_specs=(vmem, vmem, vmem),
        scratch_shapes=[
            *[pltpu.VMEM(operand.shape, operand.dtype) for operand in operands],
            pltpu.VMEM((8, 3 * CH), F32),
            pltpu.VMEM((3 * CH, 8), F32),
            pltpu.VMEM((2, A, 128 * (TAPS - 1)), BF16),
            pltpu.VMEM((3 * CH, A), BF16),
            tokens, tokens, tokens, tokens,
            pltpu.VMEM((2, CHIPS * 8, 128), F32),
            pltpu.VMEM((2 * CPG, HALF, A), BF16),
            pltpu.VMEM((4, CPG, CHIPS, A), BF16),
            pltpu.VMEM((2, CPG, CHIPS, A), BF16),
            pltpu.VMEM((2, CPG, CHIPS, A), BF16),
            tokens, tokens, tokens, tokens,
            pltpu.VMEM((ROWS, 2 * A), F32),
            pltpu.VMEM((CPG, ROWS, 2 * A), F32),
            pltpu.VMEM((ROWS, 2 * A), F32),
            pltpu.VMEM((2, ROWS, 2 * A), BF16),
            pltpu.VMEM((2, 2 * HALF, A), BF16),
            pltpu.VMEM((2 * A, 2 * A), BF16),
            pltpu.VMEM((3 * CH, A), BF16),
            pltpu.VMEM((2, 16, 3 * CH), BF16),
            pltpu.VMEM((2, 16, 3 * CH), BF16),
            pltpu.VMEM((2, 16, CH), BF16),
            pltpu.SemaphoreType.REGULAR((1,)),
            pltpu.SemaphoreType.DMA((18,)),
            pair, pair, sides, sides, pair, sides, sides, sides, sides,
            swaps, swaps, swaps, swaps,
            pltpu.SemaphoreType.DMA((4,)),
        ],
        compiler_params=pltpu.CompilerParams(collective_id=0, has_side_effects=True, vmem_limit_bytes=44 << 20),
        name="mixer",
    )(*[pltpu.with_memory_space_constraint(operand, pltpu.HBM) for operand in operands])
    mixed, proj_grad, filter_grad = write_out(mixed, proj_grad, filter_grad)
    return (mixed, proj_grad, filter_grad.reshape(1, SEQ))


def solution(mesh):
    placed = (P(None, ("dp", "ctx")), P(), P(("dp", "ctx"), None), P(None, ("dp", "ctx")))
    return jax.shard_map(
        shards,
        mesh=mesh,
        in_specs=placed,
        out_specs=(P(None, ("dp", "ctx")), P(None, ("dp", "ctx")), P(("dp", "ctx"), None)),
        check_vma=False,
    )
```
